128 devices in a mesh: sub: 32 (over y, z_hi, x), surf: 4 (over z_lo, core).
Axes of the slice: x: 4, y: 4, z: 4 (z_hi: 2, z_lo: 2; z = z_hi * 2 + z_lo), core: 2. Of those that a mesh axis runs over, the one named last changes fastest.
Arguments:
- heights: float32 [128, 512, 512], P('sub', 'surf'), may hold values from -21 to 21
- masks: int32 [4], replicated, may hold values from 1 to 31
- offsets: int32 [4, 128], replicated, may hold values from 128 to 383
- sections: int32 [128, 1], P('sub'), may hold values from 0 to 3; in each aligned block of 4 rows (0 to 3, 4 to 7, ...) at most 2 rows name the same one
- row_starts: int32 [128], P('sub'), may hold values from 0 to 888
- col_blocks: int32 [128], P('sub'), may hold values from 0 to 2
- surface: float32 [1024, 2048], P('sub', 'surf'), may hold values from -6 to 6
Outputs:
- params: float32 [4, 128], P(None, 'sub')
- fitted: float32 [1024, 2048], P('sub', 'surf')
The draws below stay inside these ranges and needn't reach their ends.
Inputs may be any that keep to these rules, and one draw needn't show every extreme that they name: `sections`: every draw has one section receiving exactly 2 subapertures of some sub index; no section receives more than 2 of one sub index.
All inputs are finite; a program needn't handle non-finite values.
Results may differ from the reference program's by a relative error of at most 0.0003.
Values sent between devices are 32-bit elements; how exact they have to be, the bound alone decides.
A program may use at most 128 MiB of HBM per device.

```python
import math
import jax
import jax.numpy as jnp
import numpy as np
from jax import lax

PIX = 512
ROUNDS = 4
SUB_DEV = 4
NCY = 1024
NCX = 2048
BLOCK = 128
CAP = 2
SUBS = 128
SEC_COLS = 512
N_SUB = 32
N_SURF = 4


def draw_heights(key, part):
    noise_key, error_key = jax.random.split(key)
    coords = (jnp.arange(PIX, dtype=jnp.float32) - (PIX - 1) * 0.5) / (PIX * 0.5)
    xgrid = coords[None, None, :]
    ygrid = coords[None, :, None]
    noise = jnp.clip(jax.random.normal(noise_key, (SUBS, PIX, PIX), jnp.float32), -6.0, 6.0)
    errors = jnp.clip(jax.random.normal(error_key, (SUBS, 4), jnp.float32), -3.0, 3.0)
    piston = errors[:, 0][:, None, None]
    tilt_x = errors[:, 1][:, None, None]
    tilt_y = errors[:, 2][:, None, None]
    power = errors[:, 3][:, None, None]
    return noise + piston + tilt_x * xgrid + tilt_y * ygrid + power * (xgrid * xgrid + ygrid * ygrid)


def touch_ends(values, key, low, largest):
    shape = values.shape
    spot = [jax.random.randint(jax.random.fold_in(key, axis), (), 0, shape[axis]) for axis in range(len(shape))]
    values = values.at[tuple(spot)].set(low)
    longest = shape.index(max(shape))
    spot[longest] = (spot[longest] + 1) % shape[longest]
    return values.at[tuple(spot)].set(largest)


def steps_of(rng, dims, cuts, low, high):
    def one(dim, blocks):
        draws = jax.random.uniform(jax.random.fold_in(jax.random.fold_in(rng, 6), dim), (blocks,), jnp.float32, low / len(cuts), high / len(cuts))
        return jnp.repeat(jnp.exp(draws), dims[dim] // blocks).reshape((-1,) + (1,) * (len(dims) - dim - 1))

    level = one(*cuts[0])
    for cut in cuts[1:]:
        level = level * one(*cut)
    return level


def shared_out(own_key, own, number, rows, amount, top, bound, slope):
    ranking = jax.random.permutation(own_key, amount)
    heavy_load, ordinary = portions_of(amount, rows * top, bound, slope, True), portions_of(amount, rows * top, bound, slope, False)
    places = jnp.arange(amount)

    def named(lengths, turn):
        used = int((lengths > 0).sum())
        fixed = max(1, used // 4)
        shifted = fixed + (places - fixed + turn * (used - fixed)) % max(1, amount - fixed)
        return jnp.zeros((amount,), jnp.int32).at[ranking[jnp.where(places < fixed, places, shifted)]].set(jnp.asarray(lengths, jnp.int32))

    lengths = jnp.where(number % 4 == 0, named(heavy_load, number // 4), named(ordinary, number - number // 4 - 1))
    mixed = jax.random.permutation(jax.random.fold_in(own, 3), amount)
    donor, sink = mixed[0:amount // 2 * 2:2], mixed[1:amount // 2 * 2:2]
    slack = jnp.minimum(lengths[donor] - 1, bound - lengths[sink]) // 2
    slack = jnp.where((donor == ranking[0]) | (sink == ranking[0]) | (lengths[sink] == 0), 0, jnp.maximum(slack, 0))
    shifted = jax.random.randint(jax.random.fold_in(own, 4), (amount // 2,), 0, 1 << 20) % (slack + 1)
    lengths = lengths.at[donor].add(-shifted).at[sink].add(shifted)
    labels = jnp.searchsorted(jnp.cumsum(lengths), jnp.arange(rows * top), side="right").astype(jnp.int32)
    table = labels.reshape(top, rows).T
    table = table[jax.random.permutation(jax.random.fold_in(own, 1), rows)]
    turn = jax.random.randint(jax.random.fold_in(own, 2), (rows, 1), 0, top)
    return jnp.take_along_axis(table, (jnp.arange(top)[None, :] + turn) % top, axis=1)


def portions_of(amount, total, bound, slope, full):
    weights = [(1 << 20) // math.isqrt(grade ** slope) + 1 for grade in range(1, amount + 1)]
    largest = bound if full else min(bound, max(-(-total // amount), total * weights[0] // sum(weights)))
    least = 1 if total - largest >= amount - 1 else 0
    counts, surplus = [largest] + [least] * (amount - 1), total - largest - least * (amount - 1)
    while surplus > 0:
        candidates = [i for i in range(1, amount) if counts[i] < largest] or [i for i in range(1, amount) if counts[i] < bound]
        pool, left = sum([weights[i] for i in candidates]), surplus
        for i in candidates:
            extra = min(bound - counts[i], max(1, left * weights[i] // pool), surplus)
            counts[i] = counts[i] + extra
            surplus = surplus - extra
    return np.array(counts)


def centred(key, dims, spread, reach, shards=(), kind=jnp.bfloat16):
    gain = steps_of(key, dims, shards, -0.22, 0.18) if shards else 1.0
    drawn = jax.random.normal(key, dims, jnp.float32) * spread * gain
    return jnp.minimum(jnp.maximum(drawn, -reach), reach).astype(kind)


def setup_inputs(seed: int = 0) -> dict:
    keys = jax.random.split(jax.random.key(seed), 8)
    heights = draw_heights(jax.random.fold_in(keys[7], 71), 0)
    masks = touch_ends(jax.random.randint(keys[1], (ROUNDS,), 1, N_SUB), jax.random.fold_in(keys[1], 1), 1, N_SUB - 1).astype(jnp.int32)
    offsets = touch_ends(jax.random.randint(keys[2], (ROUNDS, SUBS), PIX // 4, 3 * PIX // 4), jax.random.fold_in(keys[2], 1), PIX // 4, (3 * PIX // 4) - 1).astype(jnp.int32)
    sections_keys = jax.random.split(jax.random.fold_in(keys[3], 1), SUBS // SUB_DEV)
    sections_turns = jax.random.permutation(jax.random.fold_in(keys[3], 3), SUBS // SUB_DEV)
    sections = jax.vmap(lambda own, number: shared_out(jax.random.fold_in(keys[3], 2), own, number, SUB_DEV, N_SURF, 1, CAP, 2))(sections_keys, sections_turns).reshape((SUBS, 1))
    row_starts = touch_ends(jax.random.randint(keys[4], (SUBS,), 0, NCY - PIX // 4 - 7), jax.random.fold_in(keys[4], 1), 0, (NCY - PIX // 4 - 7) - 1).astype(jnp.int32)
    col_blocks = touch_ends(jax.random.randint(keys[5], (SUBS,), 0, SEC_COLS // BLOCK - 1), jax.random.fold_in(keys[5], 1), 0, (SEC_COLS // BLOCK - 1) - 1).astype(jnp.int32)
    surface = centred(keys[6], (NCY, NCX), 1.0, 6.0, ((0, 32), (1, 4)), jnp.float32)
    return {"heights": heights, "masks": masks, "offsets": offsets, "sections": sections, "row_starts": row_starts, "col_blocks": col_blocks, "surface": surface}


HIGH = lax.Precision.HIGHEST

def spline(t):
    t2 = t * t
    t3 = t2 * t
    first = t3 / 6.0
    second = (-3.0 * t3 + 12.0 * t2 - 12.0 * t + 4.0) / 6.0
    third = (3.0 * t3 - 24.0 * t2 + 60.0 * t - 44.0) / 6.0
    fourth = (4.0 - t) * (4.0 - t) * (4.0 - t) / 6.0
    inner = jnp.where(t < 1.0, first, jnp.where(t < 2.0, second, jnp.where(t < 3.0, third, fourth)))
    return jnp.where((t < 0.0) | (t >= 4.0), jnp.zeros_like(t), inner)

def spline_table(count_rows, count_cols):
    row_ids = jnp.arange(count_rows, dtype=jnp.int32).astype(jnp.float32)[:, None]
    col_ids = jnp.arange(count_cols, dtype=jnp.int32).astype(jnp.float32)[None, :]
    return spline(row_ids * 0.25 - col_ids + 3.0)

def reference(heights, masks, offsets, sections, row_starts, col_blocks, surface):
    subs = heights.shape[0]
    sub_ids = jnp.arange(subs, dtype=jnp.int32)
    owner = sub_ids // SUB_DEV
    slot = sub_ids % SUB_DEV
    coords = (jnp.arange(PIX, dtype=jnp.int32).astype(jnp.float32) - (PIX - 1) * 0.5) / (PIX * 0.5)
    xgrid = jnp.broadcast_to(coords[None, :], (PIX, PIX))
    ygrid = jnp.broadcast_to(coords[:, None], (PIX, PIX))
    basis = jnp.stack([jnp.ones((PIX, PIX), jnp.float32), xgrid, ygrid, xgrid * xgrid + ygrid * ygrid])
    cross = jnp.einsum('kyx,lyx->klx', basis, basis, precision=HIGH)
    xidx = jnp.arange(PIX, dtype=jnp.int32)
    gram = jnp.zeros((subs, 4, 4), jnp.float32)
    rhs = jnp.zeros((subs, 4), jnp.float32)
    for r in range(ROUNDS):
        partner_owner = jnp.bitwise_xor(owner, masks[r])
        partner = partner_owner * SUB_DEV + slot
        lower = owner < partner_owner
        pair = jnp.minimum(owner, partner_owner) * SUB_DEV + slot
        shift = offsets[r][pair]
        moved = jax.vmap(lambda tile, k: jnp.roll(tile, k, axis=1))(heights[partner], jnp.where(lower, shift, -shift))
        inside = jnp.where(lower[:, None], xidx[None, :] >= shift[:, None], xidx[None, :] < PIX - shift[:, None]).astype(jnp.float32)
        diff = (heights - moved) * inside[:, None, :]
        gram = gram + jnp.einsum('klx,jx->jkl', cross, inside, precision=HIGH)
        rhs = rhs + jnp.einsum('kyx,jyx->jk', basis, jnp.tanh(0.5 * diff), precision=HIGH)
    factor = jnp.linalg.cholesky(gram)
    params = jax.scipy.linalg.cho_solve((factor, True), rhs[:, :, None])[:, :, 0]
    corrected = heights - jnp.einsum('jk,kyx->jyx', params, basis, precision=HIGH)
    wide = PIX // 4 + 8
    row_table = spline_table(PIX, wide)
    col_table = spline_table(PIX, 2 * BLOCK)
    weight_rows = jnp.sum(row_table * row_table, axis=0)
    weight_cols = jnp.sum(col_table * col_table, axis=0)
    diag_piece = weight_rows[:, None] * weight_cols[None, :]
    sec_cols = NCX // N_SURF

    def add_one(i, carry):
        back_sum, diag_sum = carry
        ystart = row_starts[i].astype(jnp.int32)
        xstart = (sections[i, 0] * sec_cols + col_blocks[i] * BLOCK).astype(jnp.int32)
        window = lax.dynamic_slice(surface, (ystart, xstart), (wide, 2 * BLOCK))
        estimate = jnp.dot(jnp.dot(row_table, window, precision=HIGH), col_table.T, precision=HIGH)
        resid = corrected[i] - estimate
        back = jnp.dot(row_table.T, jnp.dot(resid, col_table, precision=HIGH), precision=HIGH)
        old = lax.dynamic_slice(back_sum, (ystart, xstart), (wide, 2 * BLOCK))
        back_sum = lax.dynamic_update_slice(back_sum, old + back, (ystart, xstart))
        old_diag = lax.dynamic_slice(diag_sum, (ystart, xstart), (wide, 2 * BLOCK))
        diag_sum = lax.dynamic_update_slice(diag_sum, old_diag + diag_piece, (ystart, xstart))
        return (back_sum, diag_sum)
    start = (jnp.zeros(surface.shape, jnp.float32), jnp.zeros(surface.shape, jnp.float32))
    back_sum, diag_sum = lax.fori_loop(0, subs, add_one, start)
    fitted = surface + back_sum / (diag_sum + 1.0)
    return (params.T, fitted)
```

```python
import functools

import jax
import jax.numpy as jnp
import ml_dtypes
import numpy as np
from jax import lax
from jax.experimental import pallas as pl
from jax.experimental.pallas import tpu as pltpu
from jax.sharding import PartitionSpec as P

HIGH = lax.Precision.HIGHEST
MESH = pl.DeviceIdType.MESH
F32 = jnp.float32
PIX = 512
ROUNDS = 4
SUBS = 128
N_SUB = 32
N_SURF = 4
WIN = 136
PART = 40
PAD = 32
TALL = WIN + 2 * PAD
BAND = 3


def spline_np(t):
    first = t**3 / 6.0
    second = (-3.0 * t**3 + 12.0 * t**2 - 12.0 * t + 4.0) / 6.0
    third = (3.0 * t**3 - 24.0 * t**2 + 60.0 * t - 44.0) / 6.0
    fourth = (4.0 - t) ** 3 / 6.0
    inner = np.where(t < 1, first, np.where(t < 2, second, np.where(t < 3, third, fourth)))
    return np.where((t < 0) | (t >= 4), 0.0, inner)


def table_np(rows, cols):
    return spline_np(np.arange(rows)[:, None] * 0.25 - np.arange(cols)[None, :] + 3.0)


COL_TABLE = np.rint(384 * table_np(PIX, 256)).astype(np.float32).astype(ml_dtypes.bfloat16)
ROW_TABLE_T = np.rint(384 * table_np(128, PART)).T.astype(np.float32).astype(ml_dtypes.bfloat16)

_FULL = table_np(PIX, 256)
_U = (np.arange(PIX) - 255.5) / 256.0
COL_NORMAL = (_FULL.T @ _FULL).astype(np.float32)
_NORMAL = _FULL.T @ _FULL
COL_SUMS = np.stack(
    [_FULL.T @ np.ones(PIX), _FULL.T @ _U, _FULL.T @ _U**2, np.diag(_NORMAL)]
).astype(np.float32)
COL_SUMS = np.concatenate([COL_SUMS, np.zeros((4, 256), np.float32)])
N_COEF = 131
_QUANT = np.zeros((N_COEF, 10))
for _a in range(N_COEF):
    for _d in range(-BAND, BAND + 1):
        if 0 <= _a + _d < N_COEF:
            _QUANT[_a, _d + BAND] = _NORMAL[_a, _a + _d]
_QUANT[:, 7:] = np.stack([_FULL.T @ np.ones(PIX), _FULL.T @ _U, _FULL.T @ _U**2], 1)[:N_COEF]
EDGES = (0, 1, 2, 128, 129, 130)
_ROW_U2 = [float((_U**k).sum()) for k in range(5)]
_MID = _QUANT[64]
_VAR = float(_MID[9] - 4.0 * ((4.0 * 63 - 255.5) / 256.0) ** 2)


def exact_dot(table, value):
    high = value.astype(jnp.bfloat16)
    low = (value - high.astype(F32)).astype(jnp.bfloat16)
    return jnp.dot(table, high, preferred_element_type=F32) + jnp.dot(
        table, low, preferred_element_type=F32
    )


def exact_dot_right(value, table):
    high = value.astype(jnp.bfloat16)
    low = (value - high.astype(F32)).astype(jnp.bfloat16)
    return jnp.dot(high, table, preferred_element_type=F32) + jnp.dot(
        low, table, preferred_element_type=F32
    )


def project_kernel(dest, h_ref, c_ref, r_ref, out_ref):
    out_ref[...] = jnp.zeros_like(out_ref)
    for j in range(4):
        wide = exact_dot_right(h_ref[j], c_ref[...])
        out_ref[dest[j]] = exact_dot(r_ref[...], wide) * (1.0 / (384.0 * 384.0))


def project(heights, dest):
    vmem = pl.BlockSpec(memory_space=pltpu.VMEM)
    return pl.pallas_call(
        project_kernel,
        out_shape=jax.ShapeDtypeStruct((8, PART, 256), F32),
        in_specs=[pl.BlockSpec(memory_space=pltpu.SMEM), vmem, vmem, vmem],
        out_specs=vmem,
        name="project",
    )(dest, heights, jnp.asarray(COL_TABLE), jnp.asarray(ROW_TABLE_T))


def gather_kernel(send_ref, meta_ref, tall_ref, metas_ref, parts, sems, own_sem):
    s, t = lax.axis_index("sub"), lax.axis_index("surf")
    x = s % 4
    base = s - x
    barrier = pltpu.get_barrier_semaphore()
    for k in range(1, 4):
        pl.semaphore_signal(
            barrier, inc=1, device_id={"sub": s, "surf": (t + k) % 4}, device_id_type=MESH
        )
        pl.semaphore_signal(
            barrier, inc=1, device_id={"sub": base + (x + k) % 4, "surf": t}, device_id_type=MESH
        )
    pl.semaphore_wait(barrier, 6)
    own = pltpu.make_async_copy(send_ref.at[t], parts.at[t], own_sem.at[0])
    own.start()
    own_meta = pltpu.make_async_copy(meta_ref, metas_ref.at[x], own_sem.at[1])
    own_meta.start()
    copies = []
    for k in range(1, 4):
        to = (t + k) % 4
        copy = pltpu.make_async_remote_copy(
            src_ref=send_ref.at[to],
            dst_ref=parts.at[t],
            send_sem=sems.at[0, k],
            recv_sem=sems.at[1, k],
            device_id={"sub": s, "surf": to},
            device_id_type=MESH,
        )
        copy.start()
        copies.append(copy)
        copy = pltpu.make_async_remote_copy(
            src_ref=meta_ref,
            dst_ref=metas_ref.at[x],
            send_sem=sems.at[2, k],
            recv_sem=sems.at[3, k],
            device_id={"sub": base + (x + k) % 4, "surf": t},
            device_id_type=MESH,
        )
        copy.start()
        copies.append(copy)
    for q in range(4):
        tall_ref[q, :, 0:PAD, :] = jnp.zeros((2, PAD, 256), F32)
        tall_ref[q, :, PAD + WIN : TALL, :] = jnp.zeros((2, PAD, 256), F32)
    own.wait()
    own_meta.wait()
    for copy in copies:
        copy.wait()
    tall_ref[x, :, PAD : PAD + WIN, :] = jnp.zeros((2, WIN, 256), F32)
    for p in range(4):
        rows = pl.ds(PAD + 32 * p, PART)
        tall_ref[x, :, rows, :] = tall_ref[x, :, rows, :] + parts[p]
    copies = []
    for k in range(1, 4):
        copy = pltpu.make_async_remote_copy(
            src_ref=tall_ref.at[x, :, pl.ds(PAD, WIN), :],
            dst_ref=tall_ref.at[x, :, pl.ds(PAD, WIN), :],
            send_sem=sems.at[4, k],
            recv_sem=sems.at[5, k],
            device_id={"sub": base + (x + k) % 4, "surf": t},
            device_id_type=MESH,
        )
        copy.start()
        copies.append(copy)
    for copy in copies:
        copy.wait()


def gather_windows(send, meta):
    vmem = pl.BlockSpec(memory_space=pltpu.VMEM)
    return pl.pallas_call(
        gather_kernel,
        out_shape=(
            jax.ShapeDtypeStruct((4, 2, TALL, 256), F32),
            jax.ShapeDtypeStruct((4, 1, 128), jnp.int32),
        ),
        in_specs=[vmem, vmem],
        out_specs=(vmem, vmem),
        scratch_shapes=[
            pltpu.VMEM((4, 2, PART, 256), F32),
            pltpu.SemaphoreType.DMA((6, 4)),
            pltpu.SemaphoreType.DMA((2,)),
        ],
        compiler_params=pltpu.CompilerParams(collective_id=0, has_side_effects=True),
        name="gather_windows",
    )(send.reshape(4, 2, PART, 256), meta)


def place_kernel(pos, tall_ref, out_ref):
    out_ref[...] = jnp.zeros_like(out_ref)
    x = pos[16]
    for w in range(8):
        start = pos[w]
        column = pl.multiple_of(pos[8 + w], 128)

        def one(b, carry, w=w, start=start, column=column):
            rel = 32 * (4 * b + x) - start

            @pl.when((rel > -32) & (rel < WIN))
            def _():
                first = rel + PAD
                base = pl.multiple_of(first // 8 * 8, 8)
                wide = tall_ref[pl.ds(w * TALL + base, 40), :]
                piece = pltpu.roll(wide, (40 - (first - base)) % 40, 0)[0:32]
                out_ref[b, :, pl.ds(column, 256)] = out_ref[b, :, pl.ds(column, 256)] + piece

            return carry

        lax.fori_loop(0, 8, one, 0)


def place(pos, tall):
    vmem = pl.BlockSpec(memory_space=pltpu.VMEM)
    return pl.pallas_call(
        place_kernel,
        out_shape=jax.ShapeDtypeStruct((8, 32, 512), F32),
        in_specs=[pl.BlockSpec(memory_space=pltpu.SMEM), vmem],
        out_specs=vmem,
        name="place",
    )(pos, tall.reshape(8 * TALL, 256))


def scatter_kernel(part_ref, surf_ref, back_ref, halo_ref, slots, sems, halo_sems):
    s, t = lax.axis_index("sub"), lax.axis_index("surf")
    x = s % 4
    b = s // 4
    up, down = (s + 1) % N_SUB, (s + N_SUB - 1) % N_SUB
    barrier = pltpu.get_barrier_semaphore()
    for k in range(1, 8):
        pl.semaphore_signal(
            barrier, inc=1, device_id={"sub": ((b + k) % 8) * 4 + x, "surf": t}, device_id_type=MESH
        )
    for to in (up, down):
        pl.semaphore_signal(barrier, inc=1, device_id={"sub": to, "surf": t}, device_id_type=MESH)
    pl.semaphore_wait(barrier, 9)
    copies = []
    for k in range(1, 8):
        to = (b + k) % 8
        copy = pltpu.make_async_remote_copy(
            src_ref=part_ref.at[to],
            dst_ref=slots.at[k],
            send_sem=sems.at[0, k],
            recv_sem=sems.at[1, k],
            device_id={"sub": to * 4 + x, "surf": t},
            device_id_type=MESH,
        )
        copy.start()
        copies.append(copy)
    for n, (to, first) in enumerate(((up, 24), (down, 0))):
        copy = pltpu.make_async_remote_copy(
            src_ref=surf_ref.at[pl.ds(first, 8), :],
            dst_ref=halo_ref.at[n],
            send_sem=halo_sems.at[0, n],
            recv_sem=halo_sems.at[1, n],
            device_id={"sub": to, "surf": t},
            device_id_type=MESH,
        )
        copy.start()
        copies.append(copy)
    for copy in copies:
        copy.wait()
    total = part_ref[b]
    for k in range(1, 8):
        total = total + slots[k]
    back_ref[...] = total


def scatter_sum(part, surface):
    vmem = pl.BlockSpec(memory_space=pltpu.VMEM)
    return pl.pallas_call(
        scatter_kernel,
        out_shape=(
            jax.ShapeDtypeStruct((32, 512), F32),
            jax.ShapeDtypeStruct((2, 8, 512), F32),
        ),
        in_specs=[vmem, vmem],
        out_specs=(vmem, vmem),
        scratch_shapes=[
            pltpu.VMEM((8, 32, 512), F32),
            pltpu.SemaphoreType.DMA((2, 8)),
            pltpu.SemaphoreType.DMA((2, 2)),
        ],
        compiler_params=pltpu.CompilerParams(collective_id=1, has_side_effects=True),
        name="scatter_sum",
    )(part, surface)


def moments_kernel(info, h_ref, recv_ref, out_ref):
    half, first_row, r = info[0], info[1], info[2]
    lower = half == 0
    xs = lax.broadcasted_iota(jnp.int32, (1, PIX), 1)
    ux = (xs.astype(F32) - 255.5) * (1.0 / 256.0)
    ys = lax.broadcasted_iota(jnp.int32, (64, 1), 0) + first_row
    uy = (ys.astype(F32) - 255.5) * (1.0 / 256.0)
    lanes = lax.broadcasted_iota(jnp.int32, (1, 128), 1)
    total = jnp.zeros((1, 128), F32)
    for j in range(4):
        shift = info[4 + j]
        padded = jnp.concatenate([recv_ref[j], jnp.zeros((64, 128), F32)], axis=1)
        moved = pltpu.roll(padded, info[8 + j], 1)
        low = jnp.where(lower, shift, 0)
        high = jnp.where(lower, PIX, PIX - shift)
        inside = (xs >= low) & (xs < high)
        value = jnp.where(inside, jnp.tanh(0.5 * (h_ref[j] - moved)), 0.0)
        value_y = value * uy
        sum0 = jnp.sum(value, axis=0, keepdims=True)
        sum1 = jnp.sum(value_y, axis=0, keepdims=True)
        sum2 = jnp.sum(value_y * uy, axis=0, keepdims=True)
        rows = (sum0, ux * sum0, sum1, ux * ux * sum0 + sum2)
        for k in range(4):
            total = jnp.where(
                lanes == 16 * j + 4 * r + k, jnp.sum(rows[k], axis=1, keepdims=True), total
            )
    out_ref[...] = total


def moments(info, heights, received):
    grid_spec = pltpu.PrefetchScalarGridSpec(
        num_scalar_prefetch=1,
        grid=(1,),
        in_specs=[
            pl.BlockSpec((4, 64, PIX), lambda i, info: (0, info[0], 0)),
            pl.BlockSpec((4, 64, 384), lambda i, info: (0, 0, 0)),
        ],
        out_specs=pl.BlockSpec((1, 128), lambda i, info: (0, 0)),
    )
    return pl.pallas_call(
        moments_kernel,
        out_shape=jax.ShapeDtypeStruct((1, 128), F32),
        grid_spec=grid_spec,
        name="moments",
    )(info, heights, received)


def share_kernel(row_ref, out_ref, parts, total, sems, far_sems, own_sem):
    s, t = lax.axis_index("sub"), lax.axis_index("surf")
    barrier = pltpu.get_barrier_semaphore()
    for k in range(1, 4):
        pl.semaphore_signal(
            barrier, inc=1, device_id={"sub": s, "surf": (t + k) % 4}, device_id_type=MESH
        )
    for k in range(1, N_SUB):
        pl.semaphore_signal(
            barrier, inc=1, device_id={"sub": (s + k) % N_SUB, "surf": t}, device_id_type=MESH
        )
    pl.semaphore_wait(barrier, 3 + N_SUB - 1)
    copies = []
    for k in range(1, 4):
        copy = pltpu.make_async_remote_copy(
            src_ref=row_ref,
            dst_ref=parts.at[k],
            send_sem=sems.at[0, k],
            recv_sem=sems.at[1, k],
            device_id={"sub": s, "surf": (t + k) % 4},
            device_id_type=MESH,
        )
        copy.start()
        copies.append(copy)
    for copy in copies:
        copy.wait()
    total[...] = (row_ref[...] + parts[1]) + (parts[2] + parts[3])
    own = pltpu.make_async_copy(total, out_ref.at[s], own_sem)
    own.start()
    copies = []
    for k in range(1, N_SUB):
        copy = pltpu.make_async_remote_copy(
            src_ref=total,
            dst_ref=out_ref.at[s],
            send_sem=far_sems.at[0, k],
            recv_sem=far_sems.at[1, k],
            device_id={"sub": (s + k) % N_SUB, "surf": t},
            device_id_type=MESH,
        )
        copy.start()
        copies.append(copy)
    own.wait()
    for copy in copies:
        copy.wait()


def share(row):
    vmem = pl.BlockSpec(memory_space=pltpu.VMEM)
    return pl.pallas_call(
        share_kernel,
        out_shape=jax.ShapeDtypeStruct((N_SUB, 1, 128), F32),
        in_specs=[vmem],
        out_specs=vmem,
        scratch_shapes=[
            pltpu.VMEM((4, 1, 128), F32),
            pltpu.VMEM((1, 128), F32),
            pltpu.SemaphoreType.DMA((2, 4)),
            pltpu.SemaphoreType.DMA((2, N_SUB)),
            pltpu.SemaphoreType.DMA,
        ],
        compiler_params=pltpu.CompilerParams(collective_id=2, has_side_effects=True),
        name="share",
    )(row)


def swap_lanes(value, width, bit, lanes):
    swapped = jnp.where(
        (lanes & width) != 0,
        pltpu.roll(value, width, 1),
        pltpu.roll(value, 128 - width, 1),
    )
    return jnp.where(bit == 1, swapped, value)


def finish_kernel(info, off_ref, m_ref, s_ref, back_ref, halo_ref, gc_ref, cs_ref, par_ref, out_ref):
    me, section = info[0], info[1]
    lane1 = lax.broadcasted_iota(jnp.int32, (1, 128), 1)
    sub1 = lane1 // 4
    rows16 = lax.broadcasted_iota(jnp.int32, (16, 128), 0)
    lane16 = lax.broadcasted_iota(jnp.int32, (16, 128), 1)
    mask16 = jnp.zeros((16, 128), jnp.int32)
    for r in range(ROUNDS):
        mask16 = jnp.where(rows16 // 4 == r, info[2 + r], mask16)
    spread = (
        lax.broadcasted_iota(jnp.int32, (N_SUB, 128), 1) // 4
        == lax.broadcasted_iota(jnp.int32, (N_SUB, 128), 0)
    ).astype(F32)
    table = lax.dot_general(
        m_ref[:, 0, :], spread, (((0,), (0,)), ((), ())), precision=HIGH, preferred_element_type=F32
    )
    own = jnp.zeros((16, 128), F32)
    place = jnp.zeros((8, 128), F32)
    for j in range(4):
        own = jnp.where(lane16 % 4 == j, table[16 * j : 16 * j + 16], own)
        place = jnp.where(lane16[:8] % 4 == j, table[64 + 8 * j : 72 + 8 * j], place)
    other = own
    shifts = off_ref[...]
    mask4 = jnp.concatenate([mask16[4 * r : 4 * r + 1] for r in range(ROUNDS)], axis=0)
    lane4 = lane16[:4]
    other_shift = shifts
    for bit in range(5):
        other = swap_lanes(other, 4 << bit, (mask16 >> bit) & 1, lane16)
        other_shift = swap_lanes(other_shift, 4 << bit, (mask4 >> bit) & 1, lane4)
    lower4 = (lane4 // 4) < jnp.bitwise_xor(lane4 // 4, mask4)
    shifts = jnp.where(lower4, shifts, other_shift)
    delta = jnp.where(lower4, shifts, -shifts).astype(F32) * (1.0 / 256.0)
    rhs = [jnp.zeros((1, 128), F32) for _ in range(4)]
    for r in range(ROUNDS):
        o = [own[4 * r + k : 4 * r + k + 1] for k in range(4)]
        p = [other[4 * r + k : 4 * r + k + 1] for k in range(4)]
        d = delta[r : r + 1]
        rhs[0] = rhs[0] + (o[0] - p[0])
        rhs[1] = rhs[1] + (o[1] - (p[1] + d * p[0]))
        rhs[2] = rhs[2] + (o[2] - p[2])
        rhs[3] = rhs[3] + (o[3] - (p[3] + d * (2.0 * p[1] + d * p[0])))
    column = lax.broadcasted_iota(jnp.int32, (PIX, 128), 0)
    count = jnp.zeros((PIX, 128), F32)
    for r in range(ROUNDS):
        shift = shifts[r : r + 1]
        low = jnp.where(lower4[r : r + 1], shift, 0)
        high = jnp.where(lower4[r : r + 1], PIX, PIX - shift)
        count = count + jnp.where((column >= low) & (column < high), 1.0, 0.0)
    ux = (lax.broadcasted_iota(jnp.int32, (PIX, 1), 0).astype(F32) - 255.5) * (1.0 / 256.0)
    power = []
    term = count
    for k in range(5):
        power.append(jnp.sum(term, axis=0, keepdims=True))
        if k < 4:
            term = term * ux
    y0, y2, y4 = _ROW_U2[0], _ROW_U2[2], _ROW_U2[4]
    g00 = power[0] * y0
    g01 = power[1] * y0
    g03 = power[2] * y0 + power[0] * y2
    g11 = power[2] * y0
    g13 = power[3] * y0 + power[1] * y2
    g22 = power[0] * y2
    g33 = power[4] * y0 + 2.0 * power[2] * y2 + power[0] * y4
    l00 = jnp.sqrt(g00)
    l10 = g01 / l00
    l30 = g03 / l00
    l11 = jnp.sqrt(g11 - l10 * l10)
    l31 = (g13 - l30 * l10) / l11
    l33 = jnp.sqrt(g33 - l30 * l30 - l31 * l31)
    z0 = rhs[0] / l00
    z1 = (rhs[1] - l10 * z0) / l11
    z3 = (rhs[3] - l30 * z0 - l31 * z1) / l33
    p3 = z3 / l33
    p1 = (z1 - l31 * p3) / l11
    p0 = (z0 - l10 * p1 - l30 * p3) / l00
    p2 = rhs[2] / g22
    params = jnp.concatenate([p0, p1, p2, p3], axis=0)
    par_ref[...] = pltpu.roll(params, (128 - 4 * me) % 128, 1)[:, 0:4]
    start = place[1:2].astype(jnp.int32)
    a = lax.broadcasted_iota(jnp.int32, (32, 128), 0) + 32 * me - start
    in_window = (a >= 0) & (a < N_COEF)
    middle = (a > EDGES[2]) & (a < EDGES[3])
    edges = [(a == e).astype(F32) for e in EDGES]

    def quantity(q, inner):
        value = jnp.where(middle, inner, 0.0)
        for e, at in zip(EDGES, edges):
            if _QUANT[e, q] != 0.0:
                value = value + at * float(_QUANT[e, q])
        return value

    centre = (4.0 * (a.astype(F32) - 1.0) - 255.5) * (1.0 / 256.0)
    bands = [quantity(q, float(_MID[q])) for q in range(7)]
    sum0 = quantity(7, 4.0)
    sum1 = quantity(8, 4.0 * centre)
    sum2 = quantity(9, 4.0 * centre * centre + _VAR)
    plane0 = p0 * sum0 + p2 * sum1 + p3 * sum2
    plane1 = p1 * sum0
    plane2 = p3 * sum0
    out_ref[...] = back_ref[...]
    weight = [jnp.zeros((32, 128), F32) for _ in range(4)]
    for c in range(3):
        chosen = (place[0:1] == section.astype(F32)) & (place[2:3] == float(c))
        chosen = chosen.astype(F32)
        band = [jnp.sum(v * chosen, axis=1, keepdims=True) for v in bands]
        plane = [jnp.sum(v * chosen, axis=1, keepdims=True) for v in (plane0, plane1, plane2)]
        cols = pl.ds(128 * c, 256)
        tall = jnp.concatenate([halo_ref[0, :, cols], s_ref[:, cols], halo_ref[1, :, cols]], axis=0)
        normal = jnp.dot(tall, gc_ref[...], precision=HIGH, preferred_element_type=F32)
        taken = plane[0] * cs_ref[0:1] + plane[1] * cs_ref[1:2] + plane[2] * cs_ref[2:3]
        for d in range(-BAND, BAND + 1):
            taken = taken + band[d + BAND] * normal[8 + d : 40 + d]
        out_ref[:, cols] = out_ref[:, cols] - taken
        diag = band[BAND] * cs_ref[3:4]
        weight[c] = weight[c] + diag[:, :128]
        weight[c + 1] = weight[c + 1] + diag[:, 128:]
    for c in range(4):
        cols = pl.ds(128 * c, 128)
        out_ref[:, cols] = s_ref[:, cols] + out_ref[:, cols] / (weight[c] + 1.0)


def finish(info, offsets, shared, surface, back, halo):
    vmem = pl.BlockSpec(memory_space=pltpu.VMEM)
    return pl.pallas_call(
        finish_kernel,
        out_shape=(jax.ShapeDtypeStruct((4, 4), F32), jax.ShapeDtypeStruct((32, 512), F32)),
        in_specs=[pl.BlockSpec(memory_space=pltpu.SMEM)] + [vmem] * 7,
        out_specs=(vmem, vmem),
        name="finish",
    )(info, offsets, shared, surface, back, halo, jnp.asarray(COL_NORMAL), jnp.asarray(COL_SUMS))


def swap_with(mask, block):
    return lax.ppermute(block, "sub", [(s, s ^ mask) for s in range(N_SUB)])


def per_device(heights, masks, offsets, sections, row_starts, col_blocks, surface):
    me_sub = lax.axis_index("sub")
    me_surf = lax.axis_index("surf")
    local = jnp.arange(4, dtype=jnp.int32)
    section_of = sections[:, 0]
    earlier = (section_of[:, None] == section_of[None, :]) & (local[None, :] < local[:, None])
    slot_of = jnp.sum(earlier.astype(jnp.int32), axis=1)
    dest = section_of * 2 + slot_of

    send = project(heights, dest)
    own_slot = (dest[None, :] == me_surf * 2 + jnp.arange(2, dtype=jnp.int32)[:, None]).astype(jnp.int32)
    slot_row = jnp.sum(own_slot * row_starts[None, :], axis=1)
    slot_col = jnp.sum(own_slot * col_blocks[None, :], axis=1) * 128
    meta = jnp.concatenate([slot_row, slot_col, jnp.zeros((124,), jnp.int32)])[None, :]
    tall, metas = gather_windows(send, meta)
    pos = jnp.concatenate(
        [metas[:, 0, 0:2].reshape(8), metas[:, 0, 2:4].reshape(8), (me_sub % 4)[None]]
    )
    part = place(pos, tall)
    back, halo = scatter_sum(part, surface)

    branches = [functools.partial(swap_with, m) for m in range(1, N_SUB)]

    def one_round(r, row):
        mask = masks[r]
        other = jnp.bitwise_xor(me_sub, mask)
        lower = me_sub < other
        half = jnp.where(lower, 0, 1)
        block = lax.dynamic_slice(heights, (0, 64 * (1 - half), 128 * (1 - half)), (4, 64, 384))
        received = lax.switch(mask - 1, branches, block)
        shift = lax.dynamic_slice(offsets, (r, jnp.minimum(me_sub, other) * 4), (1, 4))[0]
        turn = jnp.where(lower, shift, (640 - shift) % 512)
        info = jnp.concatenate(
            [jnp.stack([half, me_surf * 128 + 64 * half, r, r]), shift, turn]
        ).astype(jnp.int32)
        return row + moments(info, heights, received)

    row = lax.fori_loop(0, ROUNDS, one_round, jnp.zeros((1, 128), F32))
    places = jnp.stack([section_of, row_starts, col_blocks] + [jnp.zeros((4,), jnp.int32)] * 5, axis=1)
    places = jnp.where(me_surf == 0, places, 0).astype(F32).reshape(32)
    row = row + jnp.pad(places, (64, 32))[None, :]
    shared = share(row)
    info = jnp.concatenate([jnp.stack([me_sub, me_surf]), masks]).astype(jnp.int32)
    params, fitted = finish(info, offsets, shared, surface, back, halo)
    return params, fitted


def solution(mesh):
    in_specs = (
        P("sub", "surf", None),
        P(),
        P(),
        P("sub", None),
        P("sub"),
        P("sub"),
        P("sub", "surf"),
    )
    out_specs = (P(None, "sub"), P("sub", "surf"))
    return jax.shard_map(
        per_device, mesh=mesh, in_specs=in_specs, out_specs=out_specs, check_vma=False
    )
```

```python
import jax
import jax.numpy as jnp
import ml_dtypes
import numpy as np
from jax import lax
from jax.experimental import pallas as pl
from jax.experimental.pallas import tpu as pltpu
from jax.sharding import PartitionSpec as P

HIGH = lax.Precision.HIGHEST
MESH = pl.DeviceIdType.MESH
F32 = jnp.float32
PIX = 512
ROUNDS = 4
SUBS = 128
N_SUB = 32
N_SURF = 4
WIN = 136
PART = 40
PAD = 32
TALL = WIN + 2 * PAD
BAND = 3


def spline_np(t):
    first = t**3 / 6.0
    second = (-3.0 * t**3 + 12.0 * t**2 - 12.0 * t + 4.0) / 6.0
    third = (3.0 * t**3 - 24.0 * t**2 + 60.0 * t - 44.0) / 6.0
    fourth = (4.0 - t) ** 3 / 6.0
    inner = np.where(t < 1, first, np.where(t < 2, second, np.where(t < 3, third, fourth)))
    return np.where((t < 0) | (t >= 4), 0.0, inner)


def table_np(rows, cols):
    return spline_np(np.arange(rows)[:, None] * 0.25 - np.arange(cols)[None, :] + 3.0)


COL_TABLE = np.rint(384 * table_np(PIX, 256)).astype(np.float32).astype(ml_dtypes.bfloat16)
ROW_TABLE_T = np.rint(384 * table_np(128, PART)).T.astype(np.float32).astype(ml_dtypes.bfloat16)

_FULL = table_np(PIX, 256)
_U = (np.arange(PIX) - 255.5) / 256.0
COL_NORMAL = (_FULL.T @ _FULL).astype(np.float32)
_NORMAL = _FULL.T @ _FULL
COL_SUMS = np.stack(
    [_FULL.T @ np.ones(PIX), _FULL.T @ _U, _FULL.T @ _U**2, np.diag(_NORMAL)]
).astype(np.float32)
COL_SUMS = np.concatenate([COL_SUMS, np.zeros((4, 256), np.float32)])
N_COEF = 131
_QUANT = np.zeros((N_COEF, 10))
for _a in range(N_COEF):
    for _d in range(-BAND, BAND + 1):
        if 0 <= _a + _d < N_COEF:
            _QUANT[_a, _d + BAND] = _NORMAL[_a, _a + _d]
_QUANT[:, 7:] = np.stack([_FULL.T @ np.ones(PIX), _FULL.T @ _U, _FULL.T @ _U**2], 1)[:N_COEF]
EDGES = (0, 1, 2, 128, 129, 130)
_ROW_U2 = [float((_U**k).sum()) for k in range(5)]
_MID = _QUANT[64]
_VAR = float(_MID[9] - 4.0 * ((4.0 * 63 - 255.5) / 256.0) ** 2)


def exact_dot(table, value):
    high = value.astype(jnp.bfloat16)
    low = (value - high.astype(F32)).astype(jnp.bfloat16)
    return jnp.dot(table, high, preferred_element_type=F32) + jnp.dot(
        table, low, preferred_element_type=F32
    )


def exact_dot_right(value, table):
    high = value.astype(jnp.bfloat16)
    low = (value - high.astype(F32)).astype(jnp.bfloat16)
    return jnp.dot(high, table, preferred_element_type=F32) + jnp.dot(
        low, table, preferred_element_type=F32
    )


def project_kernel(dest, h_ref, c_ref, r_ref, out_ref):
    out_ref[...] = jnp.zeros_like(out_ref)
    for j in range(4):
        wide = exact_dot_right(h_ref[j], c_ref[...])
        out_ref[dest[j]] = exact_dot(r_ref[...], wide) * (1.0 / (384.0 * 384.0))


def project(heights, dest):
    vmem = pl.BlockSpec(memory_space=pltpu.VMEM)
    return pl.pallas_call(
        project_kernel,
        out_shape=jax.ShapeDtypeStruct((8, PART, 256), F32),
        in_specs=[pl.BlockSpec(memory_space=pltpu.SMEM), vmem, vmem, vmem],
        out_specs=vmem,
        name="project",
    )(dest, heights, jnp.asarray(COL_TABLE), jnp.asarray(ROW_TABLE_T))


def gather_kernel(send_ref, meta_ref, tall_ref, metas_ref, parts, sems, own_sem):
    s, t = lax.axis_index("sub"), lax.axis_index("surf")
    x = s % 4
    base = s - x
    barrier = pltpu.get_barrier_semaphore()
    for k in range(1, 4):
        pl.semaphore_signal(
            barrier, inc=1, device_id={"sub": s, "surf": (t + k) % 4}, device_id_type=MESH
        )
        pl.semaphore_signal(
            barrier, inc=1, device_id={"sub": base + (x + k) % 4, "surf": t}, device_id_type=MESH
        )
    pl.semaphore_wait(barrier, 6)
    own = pltpu.make_async_copy(send_ref.at[t], parts.at[t], own_sem.at[0])
    own.start()
    own_meta = pltpu.make_async_copy(meta_ref, metas_ref.at[x], own_sem.at[1])
    own_meta.start()
    copies = []
    for k in range(1, 4):
        to = (t + k) % 4
        copy = pltpu.make_async_remote_copy(
            src_ref=send_ref.at[to],
            dst_ref=parts.at[t],
            send_sem=sems.at[0, k],
            recv_sem=sems.at[1, k],
            device_id={"sub": s, "surf": to},
            device_id_type=MESH,
        )
        copy.start()
        copies.append(copy)
        copy = pltpu.make_async_remote_copy(
            src_ref=meta_ref,
            dst_ref=metas_ref.at[x],
            send_sem=sems.at[2, k],
            recv_sem=sems.at[3, k],
            device_id={"sub": base + (x + k) % 4, "surf": t},
            device_id_type=MESH,
        )
        copy.start()
        copies.append(copy)
    for q in range(4):
        tall_ref[q, :, 0:PAD, :] = jnp.zeros((2, PAD, 256), F32)
        tall_ref[q, :, PAD + WIN : TALL, :] = jnp.zeros((2, PAD, 256), F32)
    own.wait()
    own_meta.wait()
    for copy in copies:
        copy.wait()
    tall_ref[x, :, PAD : PAD + WIN, :] = jnp.zeros((2, WIN, 256), F32)
    for p in range(4):
        rows = pl.ds(PAD + 32 * p, PART)
        tall_ref[x, :, rows, :] = tall_ref[x, :, rows, :] + parts[p]
    copies = []
    for k in range(1, 4):
        copy = pltpu.make_async_remote_copy(
            src_ref=tall_ref.at[x, :, pl.ds(PAD, WIN), :],
            dst_ref=tall_ref.at[x, :, pl.ds(PAD, WIN), :],
            send_sem=sems.at[4, k],
            recv_sem=sems.at[5, k],
            device_id={"sub": base + (x + k) % 4, "surf": t},
            device_id_type=MESH,
        )
        copy.start()
        copies.append(copy)
    for copy in copies:
        copy.wait()


def gather_windows(send, meta):
    vmem = pl.BlockSpec(memory_space=pltpu.VMEM)
    return pl.pallas_call(
        gather_kernel,
        out_shape=(
            jax.ShapeDtypeStruct((4, 2, TALL, 256), F32),
            jax.ShapeDtypeStruct((4, 1, 128), jnp.int32),
        ),
        in_specs=[vmem, vmem],
        out_specs=(vmem, vmem),
        scratch_shapes=[
            pltpu.VMEM((4, 2, PART, 256), F32),
            pltpu.SemaphoreType.DMA((6, 4)),
            pltpu.SemaphoreType.DMA((2,)),
        ],
        compiler_params=pltpu.CompilerParams(collective_id=0, has_side_effects=True),
        name="gather_windows",
    )(send.reshape(4, 2, PART, 256), meta)


def place_kernel(pos, tall_ref, out_ref):
    out_ref[...] = jnp.zeros_like(out_ref)
    x = pos[16]
    for w in range(8):
        start = pos[w]
        column = pl.multiple_of(pos[8 + w], 128)

        def one(b, carry, w=w, start=start, column=column):
            rel = 32 * (4 * b + x) - start

            @pl.when((rel > -32) & (rel < WIN))
            def _():
                first = rel + PAD
                base = pl.multiple_of(first // 8 * 8, 8)
                wide = tall_ref[pl.ds(w * TALL + base, 40), :]
                piece = pltpu.roll(wide, (40 - (first - base)) % 40, 0)[0:32]
                out_ref[b, :, pl.ds(column, 256)] = out_ref[b, :, pl.ds(column, 256)] + piece

            return carry

        lax.fori_loop(0, 8, one, 0)


def place(pos, tall):
    vmem = pl.BlockSpec(memory_space=pltpu.VMEM)
    return pl.pallas_call(
        place_kernel,
        out_shape=jax.ShapeDtypeStruct((8, 32, 512), F32),
        in_specs=[pl.BlockSpec(memory_space=pltpu.SMEM), vmem],
        out_specs=vmem,
        name="place",
    )(pos, tall.reshape(8 * TALL, 256))


def scatter_kernel(part_ref, surf_ref, back_ref, halo_ref, slots, sems, halo_sems):
    s, t = lax.axis_index("sub"), lax.axis_index("surf")
    x = s % 4
    b = s // 4
    up, down = (s + 1) % N_SUB, (s + N_SUB - 1) % N_SUB
    barrier = pltpu.get_barrier_semaphore()
    for k in range(1, 8):
        pl.semaphore_signal(
            barrier, inc=1, device_id={"sub": ((b + k) % 8) * 4 + x, "surf": t}, device_id_type=MESH
        )
    for to in (up, down):
        pl.semaphore_signal(barrier, inc=1, device_id={"sub": to, "surf": t}, device_id_type=MESH)
    pl.semaphore_wait(barrier, 9)
    copies = []
    for k in range(1, 8):
        to = (b + k) % 8
        copy = pltpu.make_async_remote_copy(
            src_ref=part_ref.at[to],
            dst_ref=slots.at[k],
            send_sem=sems.at[0, k],
            recv_sem=sems.at[1, k],
            device_id={"sub": to * 4 + x, "surf": t},
            device_id_type=MESH,
        )
        copy.start()
        copies.append(copy)
    for n, (to, first) in enumerate(((up, 24), (down, 0))):
        copy = pltpu.make_async_remote_copy(
            src_ref=surf_ref.at[pl.ds(first, 8), :],
            dst_ref=halo_ref.at[n],
            send_sem=halo_sems.at[0, n],
            recv_sem=halo_sems.at[1, n],
            device_id={"sub": to, "surf": t},
            device_id_type=MESH,
        )
        copy.start()
        copies.append(copy)
    for copy in copies:
        copy.wait()
    total = part_ref[b]
    for k in range(1, 8):
        total = total + slots[k]
    back_ref[...] = total


def scatter_sum(part, surface):
    vmem = pl.BlockSpec(memory_space=pltpu.VMEM)
    return pl.pallas_call(
        scatter_kernel,
        out_shape=(
            jax.ShapeDtypeStruct((32, 512), F32),
            jax.ShapeDtypeStruct((2, 8, 512), F32),
        ),
        in_specs=[vmem, vmem],
        out_specs=(vmem, vmem),
        scratch_shapes=[
            pltpu.VMEM((8, 32, 512), F32),
            pltpu.SemaphoreType.DMA((2, 8)),
            pltpu.SemaphoreType.DMA((2, 2)),
        ],
        compiler_params=pltpu.CompilerParams(collective_id=1, has_side_effects=True),
        name="scatter_sum",
    )(part, surface)


STAGES = 5


def hop(s, kind):
    if kind == 0:
        return s + 1 - 2 * (s % 2)
    if kind == 1:
        return s + 3 - 2 * (s % 4)
    if kind == 2:
        return s + 4 - 8 * ((s // 4) % 2)
    if kind == 3:
        return s + 8 - 16 * ((s // 8) % 2)
    return s + 24 - 16 * (s // 8)


def taken(mask, kind):
    bit = [(mask >> n) & 1 for n in range(5)]
    return (bit[0] + bit[1]) % 2 if kind == 0 else (
        (bit[3] + bit[4]) % 2 if kind == 3 else bit[{1: 1, 2: 2, 4: 4}[kind]]
    )


def rounds_kernel(turns, info_ref, h_ref, place_ref, out_ref, pay, recv, parts, total, sems, near_sems, far_sems, own_sem):
    s, t = lax.axis_index("sub"), lax.axis_index("surf")
    barrier = pltpu.get_barrier_semaphore()
    for k in range(1, 4):
        pl.semaphore_signal(
            barrier, inc=1, device_id={"sub": s, "surf": (t + k) % 4}, device_id_type=MESH
        )
    for kind in range(5):
        pl.semaphore_signal(
            barrier, inc=1, device_id={"sub": hop(s, kind), "surf": t}, device_id_type=MESH
        )

    def flag(row, width):
        return info_ref[row : row + 1, 0:width] == 1

    def first(j, carry):
        for r in range(ROUNDS):
            pay[0, r, j] = jnp.where(flag(r, 384), h_ref[j, 64:128, 128:512], h_ref[j, 0:64, 0:384])
        return carry

    lax.fori_loop(0, 4, first, 0)
    pl.semaphore_wait(barrier, 8)

    def copy_of(k, r, j):
        return pltpu.make_async_remote_copy(
            src_ref=pay.at[k, r, j],
            dst_ref=recv.at[k, r, j],
            send_sem=sems.at[0, k, r, j],
            recv_sem=sems.at[1, k, r, j],
            device_id={"sub": hop(s, (k + r) % 5), "surf": t},
            device_id_type=MESH,
        )

    def begin(j, carry):
        for r in range(ROUNDS):
            copy_of(0, r, j).start()
        return carry

    lax.fori_loop(0, 4, begin, 0)
    for k in range(STAGES - 1):

        def forward(j, carry, k=k):
            for r in range(ROUNDS):
                copy_of(k, r, j).wait_recv()
                pay[k + 1, r, j] = jnp.where(
                    flag(4 + 4 * k + r, 384), recv[k, r, j], pay[k, r, j]
                )
            for r in range(ROUNDS):
                copy_of(k + 1, r, j).start()
            return carry

        lax.fori_loop(0, 4, forward, 0)

    xs = lax.broadcasted_iota(jnp.int32, (1, PIX), 1)
    ux = (xs.astype(F32) - 255.5) * (1.0 / 256.0)
    lanes = lax.broadcasted_iota(jnp.int32, (1, 128), 1)
    k = STAGES - 1

    def last(j, row):
        for r in range(ROUNDS):
            lower = flag(r, PIX)
            ys = lax.broadcasted_iota(jnp.int32, (64, 1), 0) + (128 * t + 64)
            uy = ((ys - 64 * info_ref[r : r + 1, 0:1]).astype(F32) - 255.5) * (1.0 / 256.0)
            copy_of(k, r, j).wait_recv()
            came = jnp.where(flag(4 + 4 * k + r, 384), recv[k, r, j], pay[k, r, j])
            shift = info_ref[pl.ds(24 + 4 * j + r, 1), :]
            padded = jnp.concatenate([came, jnp.zeros((64, 128), F32)], axis=1)
            moved = pltpu.roll(padded, turns[4 * r + j], 1)
            inside = jnp.where(lower, xs - shift, PIX - 1 - shift - xs) >= 0
            own = jnp.where(lower, h_ref[j, 0:64], h_ref[j, 64:128])
            value = jnp.where(inside, jnp.tanh(0.5 * (own - moved)), 0.0)
            value_y = value * uy
            sum0 = jnp.sum(value, axis=0, keepdims=True)
            sum1 = jnp.sum(value_y, axis=0, keepdims=True)
            sum2 = jnp.sum(value_y * uy, axis=0, keepdims=True)
            rows = (sum0, ux * sum0, sum1, ux * ux * sum0 + sum2)
            for q in range(4):
                row = jnp.where(
                    lanes == 16 * j + 4 * r + q, jnp.sum(rows[q], axis=1, keepdims=True), row
                )
        return row

    total[0] = lax.fori_loop(0, 4, last, place_ref[...])
    copies = []
    for n in range(1, 4):
        copy = pltpu.make_async_remote_copy(
            src_ref=total.at[0],
            dst_ref=parts.at[n],
            send_sem=near_sems.at[0, n],
            recv_sem=near_sems.at[1, n],
            device_id={"sub": s, "surf": (t + n) % 4},
            device_id_type=MESH,
        )
        copy.start()
        copies.append(copy)

    def settle(j, carry):
        for k in range(STAGES):
            for r in range(ROUNDS):
                copy_of(k, r, j).wait_send()
        return carry

    lax.fori_loop(0, 4, settle, 0)
    for copy in copies:
        copy.wait()
    total[1] = (total[0] + parts[1]) + (parts[2] + parts[3])
    own = pltpu.make_async_copy(total.at[1], out_ref.at[s], own_sem)
    own.start()

    def far(n):
        return pltpu.make_async_remote_copy(
            src_ref=total.at[1],
            dst_ref=out_ref.at[s],
            send_sem=far_sems.at[0, n],
            recv_sem=far_sems.at[1, n],
            device_id={"sub": (s + n) % N_SUB, "surf": t},
            device_id_type=MESH,
        )

    lax.fori_loop(1, N_SUB, lambda n, c: (far(n).start(), c)[1], 0)
    own.wait()
    lax.fori_loop(1, N_SUB, lambda n, c: (far(n).wait(), c)[1], 0)


def rounds(turns, info, heights, places):
    vmem = pl.BlockSpec(memory_space=pltpu.VMEM)
    return pl.pallas_call(
        rounds_kernel,
        out_shape=jax.ShapeDtypeStruct((N_SUB, 1, 128), F32),
        in_specs=[pl.BlockSpec(memory_space=pltpu.SMEM), vmem, vmem, vmem],
        out_specs=vmem,
        scratch_shapes=[
            pltpu.VMEM((STAGES, ROUNDS, 4, 64, 384), F32),
            pltpu.VMEM((STAGES, ROUNDS, 4, 64, 384), F32),
            pltpu.VMEM((4, 1, 128), F32),
            pltpu.VMEM((2, 1, 128), F32),
            pltpu.SemaphoreType.DMA((2, STAGES, ROUNDS, 4)),
            pltpu.SemaphoreType.DMA((2, 4)),
            pltpu.SemaphoreType.DMA((2, N_SUB)),
            pltpu.SemaphoreType.DMA,
        ],
        compiler_params=pltpu.CompilerParams(collective_id=2, has_side_effects=True),
        name="rounds",
    )(turns, info, heights, places)


def swap_lanes(value, width, bit, lanes):
    swapped = jnp.where(
        (lanes & width) != 0,
        pltpu.roll(value, width, 1),
        pltpu.roll(value, 128 - width, 1),
    )
    return jnp.where(bit == 1, swapped, value)


def finish_kernel(info, off_ref, m_ref, s_ref, back_ref, halo_ref, gc_ref, cs_ref, par_ref, out_ref):
    me, section = info[0], info[1]
    lane1 = lax.broadcasted_iota(jnp.int32, (1, 128), 1)
    sub1 = lane1 // 4
    rows16 = lax.broadcasted_iota(jnp.int32, (16, 128), 0)
    lane16 = lax.broadcasted_iota(jnp.int32, (16, 128), 1)
    mask16 = jnp.zeros((16, 128), jnp.int32)
    for r in range(ROUNDS):
        mask16 = jnp.where(rows16 // 4 == r, info[2 + r], mask16)
    spread = (
        lax.broadcasted_iota(jnp.int32, (N_SUB, 128), 1) // 4
        == lax.broadcasted_iota(jnp.int32, (N_SUB, 128), 0)
    ).astype(F32)
    table = lax.dot_general(
        m_ref[:, 0, :], spread, (((0,), (0,)), ((), ())), precision=HIGH, preferred_element_type=F32
    )
    own = jnp.zeros((16, 128), F32)
    place = jnp.zeros((8, 128), F32)
    for j in range(4):
        own = jnp.where(lane16 % 4 == j, table[16 * j : 16 * j + 16], own)
        place = jnp.where(lane16[:8] % 4 == j, table[64 + 8 * j : 72 + 8 * j], place)
    other = own
    shifts = off_ref[...]
    mask4 = jnp.concatenate([mask16[4 * r : 4 * r + 1] for r in range(ROUNDS)], axis=0)
    lane4 = lane16[:4]
    other_shift = shifts
    for bit in range(5):
        other = swap_lanes(other, 4 << bit, (mask16 >> bit) & 1, lane16)
        other_shift = swap_lanes(other_shift, 4 << bit, (mask4 >> bit) & 1, lane4)
    lower4 = (lane4 // 4) < jnp.bitwise_xor(lane4 // 4, mask4)
    shifts = jnp.where(lower4, shifts, other_shift)
    delta = jnp.where(lower4, shifts, -shifts).astype(F32) * (1.0 / 256.0)
    rhs = [jnp.zeros((1, 128), F32) for _ in range(4)]
    for r in range(ROUNDS):
        o = [own[4 * r + k : 4 * r + k + 1] for k in range(4)]
        p = [other[4 * r + k : 4 * r + k + 1] for k in range(4)]
        d = delta[r : r + 1]
        rhs[0] = rhs[0] + (o[0] - p[0])
        rhs[1] = rhs[1] + (o[1] - (p[1] + d * p[0]))
        rhs[2] = rhs[2] + (o[2] - p[2])
        rhs[3] = rhs[3] + (o[3] - (p[3] + d * (2.0 * p[1] + d * p[0])))
    column = lax.broadcasted_iota(jnp.int32, (PIX, 128), 0)
    count = jnp.zeros((PIX, 128), F32)
    for r in range(ROUNDS):
        shift = shifts[r : r + 1]
        low = jnp.where(lower4[r : r + 1], shift, 0)
        high = jnp.where(lower4[r : r + 1], PIX, PIX - shift)
        count = count + jnp.where((column >= low) & (column < high), 1.0, 0.0)
    ux = (lax.broadcasted_iota(jnp.int32, (PIX, 1), 0).astype(F32) - 255.5) * (1.0 / 256.0)
    power = []
    term = count
    for k in range(5):
        power.append(jnp.sum(term, axis=0, keepdims=True))
        if k < 4:
            term = term * ux
    y0, y2, y4 = _ROW_U2[0], _ROW_U2[2], _ROW_U2[4]
    g00 = power[0] * y0
    g01 = power[1] * y0
    g03 = power[2] * y0 + power[0] * y2
    g11 = power[2] * y0
    g13 = power[3] * y0 + power[1] * y2
    g22 = power[0] * y2
    g33 = power[4] * y0 + 2.0 * power[2] * y2 + power[0] * y4
    l00 = jnp.sqrt(g00)
    l10 = g01 / l00
    l30 = g03 / l00
    l11 = jnp.sqrt(g11 - l10 * l10)
    l31 = (g13 - l30 * l10) / l11
    l33 = jnp.sqrt(g33 - l30 * l30 - l31 * l31)
    z0 = rhs[0] / l00
    z1 = (rhs[1] - l10 * z0) / l11
    z3 = (rhs[3] - l30 * z0 - l31 * z1) / l33
    p3 = z3 / l33
    p1 = (z1 - l31 * p3) / l11
    p0 = (z0 - l10 * p1 - l30 * p3) / l00
    p2 = rhs[2] / g22
    params = jnp.concatenate([p0, p1, p2, p3], axis=0)
    par_ref[...] = pltpu.roll(params, (128 - 4 * me) % 128, 1)[:, 0:4]
    start = place[1:2].astype(jnp.int32)
    a = lax.broadcasted_iota(jnp.int32, (32, 128), 0) + 32 * me - start
    in_window = (a >= 0) & (a < N_COEF)
    middle = (a > EDGES[2]) & (a < EDGES[3])
    edges = [(a == e).astype(F32) for e in EDGES]

    def quantity(q, inner):
        value = jnp.where(middle, inner, 0.0)
        for e, at in zip(EDGES, edges):
            if _QUANT[e, q] != 0.0:
                value = value + at * float(_QUANT[e, q])
        return value

    centre = (4.0 * (a.astype(F32) - 1.0) - 255.5) * (1.0 / 256.0)
    bands = [quantity(q, float(_MID[q])) for q in range(7)]
    sum0 = quantity(7, 4.0)
    sum1 = quantity(8, 4.0 * centre)
    sum2 = quantity(9, 4.0 * centre * centre + _VAR)
    plane0 = p0 * sum0 + p2 * sum1 + p3 * sum2
    plane1 = p1 * sum0
    plane2 = p3 * sum0
    out_ref[...] = back_ref[...]
    weight = [jnp.zeros((32, 128), F32) for _ in range(4)]
    for c in range(3):
        chosen = (place[0:1] == section.astype(F32)) & (place[2:3] == float(c))
        chosen = chosen.astype(F32)
        band = [jnp.sum(v * chosen, axis=1, keepdims=True) for v in bands]
        plane = [jnp.sum(v * chosen, axis=1, keepdims=True) for v in (plane0, plane1, plane2)]
        cols = pl.ds(128 * c, 256)
        tall = jnp.concatenate([halo_ref[0, :, cols], s_ref[:, cols], halo_ref[1, :, cols]], axis=0)
        normal = jnp.dot(tall, gc_ref[...], precision=HIGH, preferred_element_type=F32)
        taken = plane[0] * cs_ref[0:1] + plane[1] * cs_ref[1:2] + plane[2] * cs_ref[2:3]
        for d in range(-BAND, BAND + 1):
            taken = taken + band[d + BAND] * normal[8 + d : 40 + d]
        out_ref[:, cols] = out_ref[:, cols] - taken
        diag = band[BAND] * cs_ref[3:4]
        weight[c] = weight[c] + diag[:, :128]
        weight[c + 1] = weight[c + 1] + diag[:, 128:]
    for c in range(4):
        cols = pl.ds(128 * c, 128)
        out_ref[:, cols] = s_ref[:, cols] + out_ref[:, cols] / (weight[c] + 1.0)


def finish(info, offsets, shared, surface, back, halo):
    vmem = pl.BlockSpec(memory_space=pltpu.VMEM)
    return pl.pallas_call(
        finish_kernel,
        out_shape=(jax.ShapeDtypeStruct((4, 4), F32), jax.ShapeDtypeStruct((32, 512), F32)),
        in_specs=[pl.BlockSpec(memory_space=pltpu.SMEM)] + [vmem] * 7,
        out_specs=(vmem, vmem),
        name="finish",
    )(info, offsets, shared, surface, back, halo, jnp.asarray(COL_NORMAL), jnp.asarray(COL_SUMS))


def per_device(heights, masks, offsets, sections, row_starts, col_blocks, surface):
    me_sub = lax.axis_index("sub")
    me_surf = lax.axis_index("surf")
    local = jnp.arange(4, dtype=jnp.int32)
    section_of = sections[:, 0]
    earlier = (section_of[:, None] == section_of[None, :]) & (local[None, :] < local[:, None])
    slot_of = jnp.sum(earlier.astype(jnp.int32), axis=1)
    dest = section_of * 2 + slot_of

    send = project(heights, dest)
    own_slot = (dest[None, :] == me_surf * 2 + jnp.arange(2, dtype=jnp.int32)[:, None]).astype(jnp.int32)
    slot_row = jnp.sum(own_slot * row_starts[None, :], axis=1)
    slot_col = jnp.sum(own_slot * col_blocks[None, :], axis=1) * 128
    meta = jnp.concatenate([slot_row, slot_col, jnp.zeros((124,), jnp.int32)])[None, :]
    tall, metas = gather_windows(send, meta)
    pos = jnp.concatenate(
        [metas[:, 0, 0:2].reshape(8), metas[:, 0, 2:4].reshape(8), (me_sub % 4)[None]]
    )
    part = place(pos, tall)
    back, halo = scatter_sum(part, surface)

    other = jnp.bitwise_xor(me_sub, masks)
    lower = me_sub < other
    pair = jnp.minimum(me_sub, other)[:, None] * 4 + local[None, :]
    shift = jnp.take_along_axis(offsets, pair, axis=1)
    turn = jnp.where(lower[:, None], shift, (640 - shift) % 512)
    used = jnp.stack(
        [taken(masks[r], (k + r) % 5) for k in range(STAGES) for r in range(ROUNDS)]
    )
    steps = jnp.concatenate([lower.astype(jnp.int32), used, shift.T.reshape(16)])
    steps = jnp.broadcast_to(steps[:, None], (40, PIX))
    places = jnp.stack([section_of, row_starts, col_blocks] + [jnp.zeros((4,), jnp.int32)] * 5, axis=1)
    places = jnp.where(me_surf == 0, places, 0).astype(F32).reshape(32)
    shared = rounds(turn.reshape(16), steps, heights, jnp.pad(places, (64, 32))[None, :])
    info = jnp.concatenate([jnp.stack([me_sub, me_surf]), masks]).astype(jnp.int32)
    params, fitted = finish(info, offsets, shared, surface, back, halo)
    return params, fitted


def solution(mesh):
    in_specs = (
        P("sub", "surf", None),
        P(),
        P(),
        P("sub", None),
        P("sub"),
        P("sub"),
        P("sub", "surf"),
    )
    out_specs = (P(None, "sub"), P("sub", "surf"))
    return jax.shard_map(
        per_device, mesh=mesh, in_specs=in_specs, out_specs=out_specs, check_vma=False
    )
```

```python
import jax
import jax.numpy as jnp
import ml_dtypes
import numpy as np
from jax import lax
from jax.experimental import pallas as pl
from jax.experimental.pallas import tpu as pltpu
from jax.sharding import PartitionSpec as P

HIGH = lax.Precision.HIGHEST
MESH = pl.DeviceIdType.MESH
F32 = jnp.float32
PIX = 512
ROUNDS = 4
SUBS = 128
N_SUB = 32
N_SURF = 4
WIN = 136
PART = 40
BAND = 3


def spline_np(t):
    first = t**3 / 6.0
    second = (-3.0 * t**3 + 12.0 * t**2 - 12.0 * t + 4.0) / 6.0
    third = (3.0 * t**3 - 24.0 * t**2 + 60.0 * t - 44.0) / 6.0
    fourth = (4.0 - t) ** 3 / 6.0
    inner = np.where(t < 1, first, np.where(t < 2, second, np.where(t < 3, third, fourth)))
    return np.where((t < 0) | (t >= 4), 0.0, inner)


def table_np(rows, cols):
    return spline_np(np.arange(rows)[:, None] * 0.25 - np.arange(cols)[None, :] + 3.0)


COL_TABLE = np.rint(384 * table_np(PIX, 256)).astype(np.float32).astype(ml_dtypes.bfloat16)
ROW_TABLE_T = np.rint(384 * table_np(128, PART)).T.astype(np.float32).astype(ml_dtypes.bfloat16)

_FULL = table_np(PIX, 256)
_U = (np.arange(PIX) - 255.5) / 256.0
COL_NORMAL = (_FULL.T @ _FULL).astype(np.float32)
_NORMAL = _FULL.T @ _FULL
COL_SUMS = np.stack(
    [_FULL.T @ np.ones(PIX), _FULL.T @ _U, _FULL.T @ _U**2, np.diag(_NORMAL)]
).astype(np.float32)
COL_SUMS = np.concatenate([COL_SUMS, np.zeros((4, 256), np.float32)])
N_COEF = 131
_QUANT = np.zeros((N_COEF, 10))
for _a in range(N_COEF):
    for _d in range(-BAND, BAND + 1):
        if 0 <= _a + _d < N_COEF:
            _QUANT[_a, _d + BAND] = _NORMAL[_a, _a + _d]
_QUANT[:, 7:] = np.stack([_FULL.T @ np.ones(PIX), _FULL.T @ _U, _FULL.T @ _U**2], 1)[:N_COEF]
EDGES = (0, 1, 2, 128, 129, 130)
_ROW_U2 = [float((_U**k).sum()) for k in range(5)]
_MID = _QUANT[64]
_VAR = float(_MID[9] - 4.0 * ((4.0 * 63 - 255.5) / 256.0) ** 2)


def exact_dot(table, value):
    high = value.astype(jnp.bfloat16)
    low = (value - high.astype(F32)).astype(jnp.bfloat16)
    return jnp.dot(table, high, preferred_element_type=F32) + jnp.dot(
        table, low, preferred_element_type=F32
    )


def exact_dot_right(value, table):
    high = value.astype(jnp.bfloat16)
    low = (value - high.astype(F32)).astype(jnp.bfloat16)
    return jnp.dot(high, table, preferred_element_type=F32) + jnp.dot(
        low, table, preferred_element_type=F32
    )


STAGES = 5


def hop(s, kind):
    if kind == 0:
        return s + 1 - 2 * (s % 2)
    if kind == 1:
        return s + 3 - 2 * (s % 4)
    if kind == 2:
        return s + 4 - 8 * ((s // 4) % 2)
    if kind == 3:
        return s + 8 - 16 * ((s // 8) % 2)
    return s + 24 - 16 * (s // 8)


def taken(mask, kind):
    bit = [(mask >> n) & 1 for n in range(5)]
    return (bit[0] + bit[1]) % 2 if kind == 0 else (
        (bit[3] + bit[4]) % 2 if kind == 3 else bit[{1: 1, 2: 2, 4: 4}[kind]]
    )


def setup_kernel(masks, offsets, sections, starts, blocks, info_ref, turns, place_ref):
    s, t = lax.axis_index("sub"), lax.axis_index("surf")

    def put(row, value):
        info_ref[row : row + 1] = jnp.full((1, PIX), value, jnp.int32)

    for r in range(ROUNDS):
        other = jnp.bitwise_xor(s, masks[r])
        lower = s < other
        put(r, jnp.where(lower, 1, 0))
        pair = 4 * jnp.minimum(s, other)
        for k in range(STAGES):
            put(4 + 4 * k + r, taken(masks[r], (k + r) % 5))
        for j in range(4):
            shift = offsets[r, pair + j]
            put(24 + 4 * j + r, shift)
            turns[4 * r + j] = jnp.where(lower, shift, (640 - shift) % 512)
    lanes = lax.broadcasted_iota(jnp.int32, (1, 128), 1)
    place = jnp.zeros((1, 128), jnp.int32)
    start = [jnp.int32(0), jnp.int32(0)]
    block = [jnp.int32(0), jnp.int32(0)]
    first = jnp.where(t == 0, 1, 0)
    for j in range(4):
        slot = jnp.int32(0)
        for i in range(j):
            slot = slot + jnp.where(sections[i, 0] == sections[j, 0], 1, 0)
        put(40 + j, 2 * sections[j, 0] + slot)
        for c in range(2):
            here = jnp.where((sections[j, 0] == t) & (slot == c), 1, 0)
            start[c] = start[c] + here * starts[j]
            block[c] = block[c] + here * blocks[j]
        for q, value in enumerate((sections[j, 0], starts[j], blocks[j])):
            place = jnp.where(lanes == 64 + 8 * j + q, first * value, place)
    for c in range(2):
        put(44 + c, start[c])
        put(46 + c, block[c])
    place_ref[...] = place.astype(F32)


def setup(masks, offsets, sections, starts, blocks):
    smem = pl.BlockSpec(memory_space=pltpu.SMEM)
    vmem = pl.BlockSpec(memory_space=pltpu.VMEM)
    return pl.pallas_call(
        setup_kernel,
        out_shape=(
            jax.ShapeDtypeStruct((48, PIX), jnp.int32),
            jax.ShapeDtypeStruct((16,), jnp.int32),
            jax.ShapeDtypeStruct((1, 128), F32),
        ),
        in_specs=[smem] * 5,
        out_specs=(vmem, smem, vmem),
        name="setup",
    )(masks, offsets, sections, starts, blocks)


def main_kernel(
    turns,
    info_ref,
    h_ref,
    place_ref,
    surf_ref,
    ct_ref,
    rt_ref,
    shared_ref,
    back_ref,
    halo_ref,
    pay,
    recv,
    proj,
    send,
    parts,
    win,
    metas,
    part,
    slots,
    rows_in,
    total,
    sems,
    part_sems,
    meta_sems,
    win_sems,
    sum_sems,
    halo_sems,
    near_sems,
    far_sems,
    own_sems,
):
    s, t = lax.axis_index("sub"), lax.axis_index("surf")
    x = s % 4
    base = s - x
    b = s // 4
    ring = ((s + 1) % N_SUB, (s + N_SUB - 1) % N_SUB)
    barrier = pltpu.get_barrier_semaphore()

    def greet(sub, surf):
        pl.semaphore_signal(barrier, inc=1, device_id={"sub": sub, "surf": surf}, device_id_type=MESH)

    for k in range(1, 4):
        greet(s, (t + k) % 4)
        greet(base + (x + k) % 4, t)
    for k in range(1, 8):
        greet(((b + k) % 8) * 4 + x, t)
    for to in ring:
        greet(to, t)

    def flag(row, width):
        return info_ref[row : row + 1, 0:width] == 1

    def first(j, carry):
        for r in range(ROUNDS):
            pay[0, r, j] = jnp.where(flag(r, 384), h_ref[j, 64:128, 128:512], h_ref[j, 0:64, 0:384])
        return carry

    lax.fori_loop(0, 4, first, 0)
    pl.semaphore_wait(barrier, 15)

    def remote(src, dst, pair, at, sub, surf):
        return pltpu.make_async_remote_copy(
            src_ref=src,
            dst_ref=dst,
            send_sem=pair.at[(0,) + at],
            recv_sem=pair.at[(1,) + at],
            device_id={"sub": sub, "surf": surf},
            device_id_type=MESH,
        )

    def copy_of(k, r, j):
        return remote(pay.at[k, r, j], recv.at[k, r, j], sems, (k, r, j), hop(s, (k + r) % 5), t)

    def begin(j, carry):
        for r in range(ROUNDS):
            copy_of(0, r, j).start()
        return carry

    lax.fori_loop(0, 4, begin, 0)

    def forward(k):
        def one(j, carry):
            for r in range(ROUNDS):
                copy_of(k, r, j).wait_recv()
                pay[k + 1, r, j] = jnp.where(
                    flag(4 + 4 * k + r, 384), recv[k, r, j], pay[k, r, j]
                )
            for r in range(ROUNDS):
                copy_of(k + 1, r, j).start()
            return carry

        lax.fori_loop(0, 4, one, 0)

    halos = [
        remote(surf_ref.at[pl.ds(24 - 24 * n, 8), :], halo_ref.at[n], halo_sems, (n,), ring[n], t)
        for n in range(2)
    ]
    for copy in halos:
        copy.start()

    def flatten(j, carry):
        wide = exact_dot_right(h_ref[j], ct_ref[...])
        proj[j] = exact_dot(rt_ref[...], wide) * (1.0 / (384.0 * 384.0))
        return carry

    lax.fori_loop(0, 4, flatten, 0)
    for section in range(4):
        tails = []
        for c in range(2):
            body = jnp.zeros((PART, 128), F32)
            tail = jnp.zeros((PART, 128), F32)
            for j in range(4):
                chosen = info_ref[40 + j : 41 + j, 0:128] == 2 * section + c
                body = body + jnp.where(chosen, proj[j, :, 0:128], 0.0)
                tail = tail + jnp.where(chosen, proj[j, :, 128:256], 0.0)
            send[section, c] = body
            tails.append(tail)
        send[section, 2] = tails[0] + pltpu.roll(tails[1], 64, 1)
    own_part = pltpu.make_async_copy(send.at[t], parts.at[t], own_sems.at[0])
    own_meta = pltpu.make_async_copy(
        info_ref.at[pl.ds(40, 8), pl.ds(0, 256)], metas.at[x], own_sems.at[1]
    )
    own_part.start()
    own_meta.start()
    part_copies = [
        remote(send.at[(t + k) % 4], parts.at[t], part_sems, (k,), s, (t + k) % 4)
        for k in range(1, 4)
    ]
    meta_copies = [
        remote(
            info_ref.at[pl.ds(40, 8), pl.ds(0, 256)],
            metas.at[x],
            meta_sems,
            (k,),
            base + (x + k) % 4,
            t,
        )
        for k in range(1, 4)
    ]
    for copy in part_copies + meta_copies:
        copy.start()
    forward(0)
    own_part.wait()
    own_meta.wait()
    for copy in part_copies:
        copy.wait()
    for e in range(3):
        win[x, e] = jnp.zeros((WIN, 128), F32)
        for p in range(4):
            rows = pl.ds(32 * p, PART)
            win[x, e, rows, :] = win[x, e, rows, :] + parts[p, e]
    win_copies = [
        remote(win.at[x], win.at[x], win_sems, (k,), base + (x + k) % 4, t) for k in range(1, 4)
    ]
    for copy in win_copies:
        copy.start()
    forward(1)
    for copy in meta_copies + win_copies:
        copy.wait()
    local = lax.broadcasted_iota(jnp.int32, (256, WIN), 0)
    wanted = (local // 32) * 128 + 32 * x + local % 32 - lax.broadcasted_iota(jnp.int32, (256, WIN), 1)
    narrow = lax.broadcasted_iota(jnp.int32, (WIN, 128), 1) < 64
    part[...] = jnp.zeros_like(part)

    def spread(q, carry):
        added = jnp.zeros((256, PIX), F32)
        for c in range(2):
            pick = jnp.where(wanted == metas[q, 4 + c : 5 + c, 0:WIN], 1.0, 0.0).astype(jnp.bfloat16)
            block = metas[q, 6 + c : 7 + c, 0:128]
            tail = win[q, 2] if c == 0 else pltpu.roll(win[q, 2], 64, 1)
            tail = jnp.where(narrow, tail, 0.0)
            columns = [
                jnp.where(block == n, win[q, c], 0.0) + jnp.where(block == n - 1, tail, 0.0)
                for n in range(4)
            ]
            added = added + exact_dot(pick, jnp.concatenate(columns, axis=1))
        part[...] = part[...] + added.reshape(8, 32, PIX)
        return carry

    lax.fori_loop(0, 4, spread, 0)
    sum_copies = [
        remote(part.at[(b + k) % 8], slots.at[k], sum_sems, (k,), ((b + k) % 8) * 4 + x, t)
        for k in range(1, 8)
    ]
    for copy in sum_copies:
        copy.start()
    forward(2)
    forward(3)

    xs = lax.broadcasted_iota(jnp.int32, (1, PIX), 1)
    ux = (xs.astype(F32) - 255.5) * (1.0 / 256.0)
    lanes = lax.broadcasted_iota(jnp.int32, (1, 128), 1)
    k = STAGES - 1

    def last(j, row):
        for r in range(ROUNDS):
            lower = flag(r, PIX)
            ys = lax.broadcasted_iota(jnp.int32, (64, 1), 0) + (128 * t + 64)
            uy = ((ys - 64 * info_ref[r : r + 1, 0:1]).astype(F32) - 255.5) * (1.0 / 256.0)
            copy_of(k, r, j).wait_recv()
            came = jnp.where(flag(4 + 4 * k + r, 384), recv[k, r, j], pay[k, r, j])
            shift = info_ref[pl.ds(24 + 4 * j + r, 1), :]
            padded = jnp.concatenate([came, jnp.zeros((64, 128), F32)], axis=1)
            moved = pltpu.roll(padded, turns[4 * r + j], 1)
            inside = jnp.where(lower, xs - shift, PIX - 1 - shift - xs) >= 0
            own = jnp.where(lower, h_ref[j, 0:64], h_ref[j, 64:128])
            value = jnp.where(inside, jnp.tanh(0.5 * (own - moved)), 0.0)
            value_y = value * uy
            sum0 = jnp.sum(value, axis=0, keepdims=True)
            sum1 = jnp.sum(value_y, axis=0, keepdims=True)
            sum2 = jnp.sum(value_y * uy, axis=0, keepdims=True)
            rows = (sum0, ux * sum0, sum1, ux * ux * sum0 + sum2)
            for q in range(4):
                row = jnp.where(
                    lanes == 16 * j + 4 * r + q, jnp.sum(rows[q], axis=1, keepdims=True), row
                )
        return row

    total[0] = lax.fori_loop(0, 4, last, place_ref[...])
    near = [
        remote(total.at[0], rows_in.at[n], near_sems, (n,), s, (t + n) % 4) for n in range(1, 4)
    ]
    for copy in near:
        copy.start()

    def settle(j, carry):
        for k in range(STAGES):
            for r in range(ROUNDS):
                copy_of(k, r, j).wait_send()
        return carry

    lax.fori_loop(0, 4, settle, 0)
    for copy in near:
        copy.wait()
    total[1] = (total[0] + rows_in[1]) + (rows_in[2] + rows_in[3])
    own = pltpu.make_async_copy(total.at[1], shared_ref.at[s], own_sems.at[2])
    own.start()

    def far(n):
        return remote(total.at[1], shared_ref.at[s], far_sems, (n,), (s + n) % N_SUB, t)

    lax.fori_loop(1, N_SUB, lambda n, c: (far(n).start(), c)[1], 0)
    for copy in sum_copies + halos:
        copy.wait()
    summed = part[b]
    for n in range(1, 8):
        summed = summed + slots[n]
    back_ref[...] = summed
    own.wait()
    lax.fori_loop(1, N_SUB, lambda n, c: (far(n).wait(), c)[1], 0)


def main(turns, info, heights, places, surface):
    smem = pl.BlockSpec(memory_space=pltpu.SMEM)
    vmem = pl.BlockSpec(memory_space=pltpu.VMEM)
    dma = pltpu.SemaphoreType.DMA
    return pl.pallas_call(
        main_kernel,
        out_shape=(
            jax.ShapeDtypeStruct((N_SUB, 1, 128), F32),
            jax.ShapeDtypeStruct((32, PIX), F32),
            jax.ShapeDtypeStruct((2, 8, PIX), F32),
        ),
        in_specs=[smem] + [vmem] * 6,
        out_specs=(vmem, vmem, vmem),
        scratch_shapes=[
            pltpu.VMEM((STAGES, ROUNDS, 4, 64, 384), F32),
            pltpu.VMEM((STAGES, ROUNDS, 4, 64, 384), F32),
            pltpu.VMEM((4, PART, 256), F32),
            pltpu.VMEM((4, 3, PART, 128), F32),
            pltpu.VMEM((4, 3, PART, 128), F32),
            pltpu.VMEM((4, 3, WIN, 128), F32),
            pltpu.VMEM((4, 8, 256), jnp.int32),
            pltpu.VMEM((8, 32, PIX), F32),
            pltpu.VMEM((8, 32, PIX), F32),
            pltpu.VMEM((4, 1, 128), F32),
            pltpu.VMEM((2, 1, 128), F32),
            dma((2, STAGES, ROUNDS, 4)),
            dma((2, 4)),
            dma((2, 4)),
            dma((2, 4)),
            dma((2, 8)),
            dma((2, 2)),
            dma((2, 4)),
            dma((2, N_SUB)),
            dma((3,)),
        ],
        compiler_params=pltpu.CompilerParams(collective_id=0, has_side_effects=True),
        name="main",
    )(turns, info, heights, places, surface, jnp.asarray(COL_TABLE), jnp.asarray(ROW_TABLE_T))


def swap_lanes(value, width, bit, lanes):
    swapped = jnp.where(
        (lanes & width) != 0,
        pltpu.roll(value, width, 1),
        pltpu.roll(value, 128 - width, 1),
    )
    return jnp.where(bit == 1, swapped, value)


def finish_kernel(masks, off_ref, m_ref, s_ref, back_ref, halo_ref, gc_ref, cs_ref, par_ref, out_ref):
    me, section = lax.axis_index("sub"), lax.axis_index("surf")
    lane1 = lax.broadcasted_iota(jnp.int32, (1, 128), 1)
    sub1 = lane1 // 4
    rows16 = lax.broadcasted_iota(jnp.int32, (16, 128), 0)
    lane16 = lax.broadcasted_iota(jnp.int32, (16, 128), 1)
    mask16 = jnp.zeros((16, 128), jnp.int32)
    for r in range(ROUNDS):
        mask16 = jnp.where(rows16 // 4 == r, masks[r], mask16)
    spread = (
        lax.broadcasted_iota(jnp.int32, (N_SUB, 128), 1) // 4
        == lax.broadcasted_iota(jnp.int32, (N_SUB, 128), 0)
    ).astype(F32)
    table = lax.dot_general(
        m_ref[:, 0, :], spread, (((0,), (0,)), ((), ())), precision=HIGH, preferred_element_type=F32
    )
    own = jnp.zeros((16, 128), F32)
    place = jnp.zeros((8, 128), F32)
    for j in range(4):
        own = jnp.where(lane16 % 4 == j, table[16 * j : 16 * j + 16], own)
        place = jnp.where(lane16[:8] % 4 == j, table[64 + 8 * j : 72 + 8 * j], place)
    other = own
    shifts = off_ref[...]
    mask4 = jnp.concatenate([mask16[4 * r : 4 * r + 1] for r in range(ROUNDS)], axis=0)
    lane4 = lane16[:4]
    other_shift = shifts
    for bit in range(5):
        other = swap_lanes(other, 4 << bit, (mask16 >> bit) & 1, lane16)
        other_shift = swap_lanes(other_shift, 4 << bit, (mask4 >> bit) & 1, lane4)
    lower4 = (lane4 // 4) < jnp.bitwise_xor(lane4 // 4, mask4)
    shifts = jnp.where(lower4, shifts, other_shift)
    delta = jnp.where(lower4, shifts, -shifts).astype(F32) * (1.0 / 256.0)
    rhs = [jnp.zeros((1, 128), F32) for _ in range(4)]
    for r in range(ROUNDS):
        o = [own[4 * r + k : 4 * r + k + 1] for k in range(4)]
        p = [other[4 * r + k : 4 * r + k + 1] for k in range(4)]
        d = delta[r : r + 1]
        rhs[0] = rhs[0] + (o[0] - p[0])
        rhs[1] = rhs[1] + (o[1] - (p[1] + d * p[0]))
        rhs[2] = rhs[2] + (o[2] - p[2])
        rhs[3] = rhs[3] + (o[3] - (p[3] + d * (2.0 * p[1] + d * p[0])))
    column = lax.broadcasted_iota(jnp.int32, (PIX, 128), 0)
    count = jnp.zeros((PIX, 128), F32)
    for r in range(ROUNDS):
        shift = shifts[r : r + 1]
        low = jnp.where(lower4[r : r + 1], shift, 0)
        high = jnp.where(lower4[r : r + 1], PIX, PIX - shift)
        count = count + jnp.where((column >= low) & (column < high), 1.0, 0.0)
    ux = (lax.broadcasted_iota(jnp.int32, (PIX, 1), 0).astype(F32) - 255.5) * (1.0 / 256.0)
    power = []
    term = count
    for k in range(5):
        power.append(jnp.sum(term, axis=0, keepdims=True))
        if k < 4:
            term = term * ux
    y0, y2, y4 = _ROW_U2[0], _ROW_U2[2], _ROW_U2[4]
    g00 = power[0] * y0
    g01 = power[1] * y0
    g03 = power[2] * y0 + power[0] * y2
    g11 = power[2] * y0
    g13 = power[3] * y0 + power[1] * y2
    g22 = power[0] * y2
    g33 = power[4] * y0 + 2.0 * power[2] * y2 + power[0] * y4
    l00 = jnp.sqrt(g00)
    l10 = g01 / l00
    l30 = g03 / l00
    l11 = jnp.sqrt(g11 - l10 * l10)
    l31 = (g13 - l30 * l10) / l11
    l33 = jnp.sqrt(g33 - l30 * l30 - l31 * l31)
    z0 = rhs[0] / l00
    z1 = (rhs[1] - l10 * z0) / l11
    z3 = (rhs[3] - l30 * z0 - l31 * z1) / l33
    p3 = z3 / l33
    p1 = (z1 - l31 * p3) / l11
    p0 = (z0 - l10 * p1 - l30 * p3) / l00
    p2 = rhs[2] / g22
    params = jnp.concatenate([p0, p1, p2, p3], axis=0)
    par_ref[...] = pltpu.roll(params, (128 - 4 * me) % 128, 1)[:, 0:4]
    start = place[1:2].astype(jnp.int32)
    a = lax.broadcasted_iota(jnp.int32, (32, 128), 0) + 32 * me - start
    in_window = (a >= 0) & (a < N_COEF)
    middle = (a > EDGES[2]) & (a < EDGES[3])
    edges = [(a == e).astype(F32) for e in EDGES]

    def quantity(q, inner):
        value = jnp.where(middle, inner, 0.0)
        for e, at in zip(EDGES, edges):
            if _QUANT[e, q] != 0.0:
                value = value + at * float(_QUANT[e, q])
        return value

    centre = (4.0 * (a.astype(F32) - 1.0) - 255.5) * (1.0 / 256.0)
    bands = [quantity(q, float(_MID[q])) for q in range(7)]
    sum0 = quantity(7, 4.0)
    sum1 = quantity(8, 4.0 * centre)
    sum2 = quantity(9, 4.0 * centre * centre + _VAR)
    plane0 = p0 * sum0 + p2 * sum1 + p3 * sum2
    plane1 = p1 * sum0
    plane2 = p3 * sum0
    out_ref[...] = back_ref[...]
    weight = [jnp.zeros((32, 128), F32) for _ in range(4)]
    for c in range(3):
        chosen = (place[0:1] == section.astype(F32)) & (place[2:3] == float(c))
        chosen = chosen.astype(F32)
        band = [jnp.sum(v * chosen, axis=1, keepdims=True) for v in bands]
        plane = [jnp.sum(v * chosen, axis=1, keepdims=True) for v in (plane0, plane1, plane2)]
        cols = pl.ds(128 * c, 256)
        tall = jnp.concatenate([halo_ref[0, :, cols], s_ref[:, cols], halo_ref[1, :, cols]], axis=0)
        normal = jnp.dot(tall, gc_ref[...], precision=HIGH, preferred_element_type=F32)
        taken = plane[0] * cs_ref[0:1] + plane[1] * cs_ref[1:2] + plane[2] * cs_ref[2:3]
        for d in range(-BAND, BAND + 1):
            taken = taken + band[d + BAND] * normal[8 + d : 40 + d]
        out_ref[:, cols] = out_ref[:, cols] - taken
        diag = band[BAND] * cs_ref[3:4]
        weight[c] = weight[c] + diag[:, :128]
        weight[c + 1] = weight[c + 1] + diag[:, 128:]
    for c in range(4):
        cols = pl.ds(128 * c, 128)
        out_ref[:, cols] = s_ref[:, cols] + out_ref[:, cols] / (weight[c] + 1.0)


def finish(masks, offsets, shared, surface, back, halo):
    vmem = pl.BlockSpec(memory_space=pltpu.VMEM)
    return pl.pallas_call(
        finish_kernel,
        out_shape=(jax.ShapeDtypeStruct((4, 4), F32), jax.ShapeDtypeStruct((32, 512), F32)),
        in_specs=[pl.BlockSpec(memory_space=pltpu.SMEM)] + [vmem] * 7,
        out_specs=(vmem, vmem),
        name="finish",
    )(masks, offsets, shared, surface, back, halo, jnp.asarray(COL_NORMAL), jnp.asarray(COL_SUMS))


def per_device(heights, masks, offsets, sections, row_starts, col_blocks, surface):
    info, turns, places = setup(masks, offsets, sections, row_starts, col_blocks)
    shared, back, halo = main(turns, info, heights, places, surface)
    params, fitted = finish(masks, offsets, shared, surface, back, halo)
    return params, fitted


def solution(mesh):
    in_specs = (
        P("sub", "surf", None),
        P(),
        P(),
        P("sub", None),
        P("sub"),
        P("sub"),
        P("sub", "surf"),
    )
    out_specs = (P(None, "sub"), P("sub", "surf"))
    return jax.shard_map(
        per_device, mesh=mesh, in_specs=in_specs, out_specs=out_specs, check_vma=False
    )
```

```python
import functools

import jax
import jax.numpy as jnp
import ml_dtypes
import numpy as np
from jax import lax
from jax.experimental import pallas as pl
from jax.experimental.pallas import tpu as pltpu
from jax.sharding import PartitionSpec as P

HIGH = lax.Precision.HIGHEST
MESH = pl.DeviceIdType.MESH
F32 = jnp.float32
PIX = 512
ROUNDS = 4
SUBS = 128
N_SUB = 32
N_SURF = 4
WIN = 136
PART = 40
BAND = 3


def spline_np(t):
    first = t**3 / 6.0
    second = (-3.0 * t**3 + 12.0 * t**2 - 12.0 * t + 4.0) / 6.0
    third = (3.0 * t**3 - 24.0 * t**2 + 60.0 * t - 44.0) / 6.0
    fourth = (4.0 - t) ** 3 / 6.0
    inner = np.where(t < 1, first, np.where(t < 2, second, np.where(t < 3, third, fourth)))
    return np.where((t < 0) | (t >= 4), 0.0, inner)


def table_np(rows, cols):
    return spline_np(np.arange(rows)[:, None] * 0.25 - np.arange(cols)[None, :] + 3.0)


COL_TABLE = np.rint(384 * table_np(PIX, 256)).astype(np.float32).astype(ml_dtypes.bfloat16)
ROW_TABLE_T = np.rint(384 * table_np(128, PART)).T.astype(np.float32).astype(ml_dtypes.bfloat16)

_FULL = table_np(PIX, 256)
_U = (np.arange(PIX) - 255.5) / 256.0
COL_NORMAL = (_FULL.T @ _FULL).astype(np.float32)
_NORMAL = _FULL.T @ _FULL
COL_SUMS = np.stack(
    [_FULL.T @ np.ones(PIX), _FULL.T @ _U, _FULL.T @ _U**2, np.diag(_NORMAL)]
).astype(np.float32)
COL_SUMS = np.concatenate([COL_SUMS, np.zeros((4, 256), np.float32)])
N_COEF = 131
_QUANT = np.zeros((N_COEF, 10))
for _a in range(N_COEF):
    for _d in range(-BAND, BAND + 1):
        if 0 <= _a + _d < N_COEF:
            _QUANT[_a, _d + BAND] = _NORMAL[_a, _a + _d]
_QUANT[:, 7:] = np.stack([_FULL.T @ np.ones(PIX), _FULL.T @ _U, _FULL.T @ _U**2], 1)[:N_COEF]
EDGES = (0, 1, 2, 128, 129, 130)
_ROW_U2 = [float((_U**k).sum()) for k in range(5)]
_MID = _QUANT[64]
_VAR = float(_MID[9] - 4.0 * ((4.0 * 63 - 255.5) / 256.0) ** 2)


def exact_dot(table, value):
    high = value.astype(jnp.bfloat16)
    low = (value - high.astype(F32)).astype(jnp.bfloat16)
    return jnp.dot(table, high, preferred_element_type=F32) + jnp.dot(
        table, low, preferred_element_type=F32
    )


def exact_dot_right(value, table):
    high = value.astype(jnp.bfloat16)
    low = (value - high.astype(F32)).astype(jnp.bfloat16)
    return jnp.dot(high, table, preferred_element_type=F32) + jnp.dot(
        low, table, preferred_element_type=F32
    )


STAGES = 5
STREAMS = ((0, 24), (24, 24), (48, 24), (72, 24), (96, 32), (128, 24), (152, 24), (176, 24), (200, 24), (224, 32))


def hop(s, kind):
    if kind == 0:
        return s + 1 - 2 * (s % 2)
    if kind == 1:
        return s + 3 - 2 * (s % 4)
    if kind == 2:
        return s + 4 - 8 * ((s // 4) % 2)
    if kind == 3:
        return s + 8 - 16 * ((s // 8) % 2)
    return s + 24 - 16 * (s // 8)


def taken(mask, kind):
    bit = [(mask >> n) & 1 for n in range(5)]
    return (bit[0] + bit[1]) % 2 if kind == 0 else (
        (bit[3] + bit[4]) % 2 if kind == 3 else bit[{1: 1, 2: 2, 4: 4}[kind]]
    )


def setup_kernel(masks, offsets, sections, starts, blocks, info_ref, turns, place_ref, fits_ref):
    s, t = lax.axis_index("sub"), lax.axis_index("surf")

    def put(row, value):
        info_ref[row : row + 1] = jnp.full((1, PIX), value, jnp.int32)

    for r in range(ROUNDS):
        other = jnp.bitwise_xor(s, masks[r])
        lower = s < other
        put(r, jnp.where(lower, 1, 0))
        pair = 4 * jnp.minimum(s, other)
        for kind in range(STAGES):
            put(4 + 4 * kind + r, taken(masks[r], kind))
        for j in range(4):
            shift = offsets[r, pair + j]
            put(24 + 4 * j + r, shift)
            turns[4 * r + j] = jnp.where(lower, shift, (640 - shift) % 512)
    fits = jnp.int32(1)
    for kind in range(STAGES):
        need = [taken(masks[r], kind) for r in range(ROUNDS)]
        rest = need[3]
        for n in range(3):
            put(48 + 3 * kind + n, rest * (1 - need[n]))
            rest = rest * need[n]
        fits = fits * (1 - rest)
    fits_ref[0] = fits
    lanes = lax.broadcasted_iota(jnp.int32, (1, 128), 1)
    place = jnp.zeros((1, 128), jnp.int32)
    start = [jnp.int32(0), jnp.int32(0)]
    block = [jnp.int32(0), jnp.int32(0)]
    first = jnp.where(t == 0, 1, 0)
    for j in range(4):
        slot = jnp.int32(0)
        for i in range(j):
            slot = slot + jnp.where(sections[i] == sections[j], 1, 0)
        put(40 + j, 2 * sections[j] + slot)
        for c in range(2):
            here = jnp.where((sections[j] == t) & (slot == c), 1, 0)
            start[c] = start[c] + here * starts[j]
            block[c] = block[c] + here * blocks[j]
        for q, value in enumerate((sections[j], starts[j], blocks[j])):
            place = jnp.where(lanes == 64 + 8 * j + q, first * value, place)
    for c in range(2):
        put(44 + c, start[c])
        put(46 + c, block[c])
    place_ref[...] = place.astype(F32)


def setup(masks, offsets, sections, starts, blocks):
    smem = pl.BlockSpec(memory_space=pltpu.SMEM)
    vmem = pl.BlockSpec(memory_space=pltpu.VMEM)
    return pl.pallas_call(
        setup_kernel,
        out_shape=(
            jax.ShapeDtypeStruct((64, PIX), jnp.int32),
            jax.ShapeDtypeStruct((16,), jnp.int32),
            jax.ShapeDtypeStruct((1, 128), F32),
            jax.ShapeDtypeStruct((1,), jnp.int32),
        ),
        in_specs=[smem] * 5,
        out_specs=(vmem, smem, vmem, smem),
        name="setup",
    )(masks, offsets, sections, starts, blocks)


def main_kernel(
    count,
    turns,
    info_ref,
    h_ref,
    place_ref,
    surf_ref,
    ct_ref,
    rt_ref,
    shared_ref,
    back_ref,
    halo_ref,
    pay,
    outs,
    recv,
    proj,
    send,
    parts,
    win,
    metas,
    part,
    slots,
    rows_in,
    total,
    sems,
    part_sems,
    meta_sems,
    win_sems,
    sum_sems,
    halo_sems,
    near_sems,
    far_sems,
    own_sems,
):
    s, t = lax.axis_index("sub"), lax.axis_index("surf")
    x = s % 4
    base = s - x
    b = s // 4
    ring = ((s + 1) % N_SUB, (s + N_SUB - 1) % N_SUB)
    barrier = pltpu.get_barrier_semaphore()

    def greet(sub, surf):
        pl.semaphore_signal(barrier, inc=1, device_id={"sub": sub, "surf": surf}, device_id_type=MESH)

    for k in range(1, 4):
        greet(s, (t + k) % 4)
        greet(base + (x + k) % 4, t)
    for k in range(1, 8):
        greet(((b + k) % 8) * 4 + x, t)
    for to in ring:
        greet(to, t)

    def flag(row, width):
        return info_ref[row : row + 1, 0:width] == 1

    for r in range(ROUNDS):
        for j in range(4):
            pay[r, 64 * j : 64 * j + 64] = jnp.where(
                flag(r, 384), h_ref[j, 64:128, 128:512], h_ref[j, 0:64, 0:384]
            )

    def load(k, q):
        first, size = STREAMS[q]
        rows = pl.ds(first, size)
        for n in range(count):
            value = pay[n, rows, :]
            if count < ROUNDS:
                value = jnp.where(flag(48 + 3 * ((k + q) % 5) + n, 384), pay[3, rows, :], value)
            outs[k, pl.ds(count * first + n * size, size), :] = value

    for q in range(10):
        load(0, q)
    pl.semaphore_wait(barrier, 15)

    def remote(src, dst, pair, at, sub, surf):
        return pltpu.make_async_remote_copy(
            src_ref=src,
            dst_ref=dst,
            send_sem=pair.at[(0,) + at],
            recv_sem=pair.at[(1,) + at],
            device_id={"sub": sub, "surf": surf},
            device_id_type=MESH,
        )

    def copy_of(k, q):
        first, size = STREAMS[q]
        rows = pl.ds(count * first, count * size)
        return remote(
            outs.at[k, rows, :], recv.at[k, rows, :], sems, (k, q), hop(s, (k + q) % 5), t
        )

    for q in range(10):
        copy_of(0, q).start()

    def take(k, q):
        first, size = STREAMS[q]
        rows = pl.ds(first, size)
        kind = (k + q) % 5
        copy_of(k, q).wait_recv()
        came = [recv[k, pl.ds(count * first + n * size, size), :] for n in range(count)]
        for n in range(count):
            pay[n, rows, :] = jnp.where(flag(4 + 4 * kind + n, 384), came[n], pay[n, rows, :])
        if count < ROUNDS:
            extra = pay[3, rows, :]
            for n in range(count):
                extra = jnp.where(flag(48 + 3 * kind + n, 384), came[n], extra)
            pay[3, rows, :] = extra

    def forward(k):
        for q in sorted(range(10), key=lambda q: (q // 5, (k + q) % 5 == 2)):
            take(k, q)
            load(k + 1, q)
            copy_of(k + 1, q).start()

    halos = [
        remote(surf_ref.at[pl.ds(24 - 24 * n, 8), :], halo_ref.at[n], halo_sems, (n,), ring[n], t)
        for n in range(2)
    ]
    for copy in halos:
        copy.start()

    def flatten(j, carry):
        wide = exact_dot_right(h_ref[j], ct_ref[...])
        proj[j] = exact_dot(rt_ref[...], wide) * (1.0 / (384.0 * 384.0))
        return carry

    lax.fori_loop(0, 4, flatten, 0)
    for section in range(4):
        tails = []
        for c in range(2):
            body = jnp.zeros((PART, 128), F32)
            tail = jnp.zeros((PART, 128), F32)
            for j in range(4):
                chosen = info_ref[40 + j : 41 + j, 0:128] == 2 * section + c
                body = body + jnp.where(chosen, proj[j, :, 0:128], 0.0)
                tail = tail + jnp.where(chosen, proj[j, :, 128:256], 0.0)
            send[section, c] = body
            tails.append(tail)
        send[section, 2] = tails[0] + pltpu.roll(tails[1], 64, 1)
    own_part = pltpu.make_async_copy(send.at[t], parts.at[t], own_sems.at[0])
    own_meta = pltpu.make_async_copy(
        info_ref.at[pl.ds(40, 8), pl.ds(0, 256)], metas.at[x], own_sems.at[1]
    )
    own_part.start()
    own_meta.start()
    part_copies = [
        remote(send.at[(t + k) % 4], parts.at[t], part_sems, (k,), s, (t + k) % 4)
        for k in range(1, 4)
    ]
    meta_copies = [
        remote(
            info_ref.at[pl.ds(40, 8), pl.ds(0, 256)],
            metas.at[x],
            meta_sems,
            (k,),
            base + (x + k) % 4,
            t,
        )
        for k in range(1, 4)
    ]
    for copy in part_copies + meta_copies:
        copy.start()
    forward(0)
    own_part.wait()
    own_meta.wait()
    for copy in part_copies:
        copy.wait()
    for e in range(3):
        win[x, e] = jnp.zeros((WIN, 128), F32)
        for p in range(4):
            rows = pl.ds(32 * p, PART)
            win[x, e, rows, :] = win[x, e, rows, :] + parts[p, e]
    win_copies = [
        remote(win.at[x], win.at[x], win_sems, (k,), base + (x + k) % 4, t) for k in range(1, 4)
    ]
    for copy in win_copies:
        copy.start()
    forward(1)
    forward(2)
    for copy in meta_copies + win_copies:
        copy.wait()
    local = lax.broadcasted_iota(jnp.int32, (256, WIN), 0)
    wanted = (local // 32) * 128 + 32 * x + local % 32 - lax.broadcasted_iota(jnp.int32, (256, WIN), 1)
    narrow = lax.broadcasted_iota(jnp.int32, (WIN, 128), 1) < 64
    part[...] = jnp.zeros_like(part)

    def spread(q, carry):
        added = jnp.zeros((256, PIX), F32)
        for c in range(2):
            pick = jnp.where(wanted == metas[q, 4 + c : 5 + c, 0:WIN], 1.0, 0.0).astype(jnp.bfloat16)
            block = metas[q, 6 + c : 7 + c, 0:128]
            tail = win[q, 2] if c == 0 else pltpu.roll(win[q, 2], 64, 1)
            tail = jnp.where(narrow, tail, 0.0)
            columns = [
                jnp.where(block == n, win[q, c], 0.0) + jnp.where(block == n - 1, tail, 0.0)
                for n in range(4)
            ]
            added = added + exact_dot(pick, jnp.concatenate(columns, axis=1))
        part[...] = part[...] + added.reshape(8, 32, PIX)
        return carry

    lax.fori_loop(0, 4, spread, 0)
    sum_copies = [
        remote(part.at[(b + k) % 8], slots.at[k], sum_sems, (k,), ((b + k) % 8) * 4 + x, t)
        for k in range(1, 8)
    ]
    for copy in sum_copies:
        copy.start()
    forward(3)

    xs = lax.broadcasted_iota(jnp.int32, (1, PIX), 1)
    ux = (xs.astype(F32) - 255.5) * (1.0 / 256.0)
    lanes = lax.broadcasted_iota(jnp.int32, (1, 128), 1)
    row = place_ref[...]
    done = 0
    for j in range(4):
        while done < 10 and STREAMS[done][0] < 64 * j + 64:
            take(STAGES - 1, done)
            done += 1
        for r in range(ROUNDS):
            lower = flag(r, PIX)
            ys = lax.broadcasted_iota(jnp.int32, (64, 1), 0) + (128 * t + 64)
            uy = ((ys - 64 * info_ref[r : r + 1, 0:1]).astype(F32) - 255.5) * (1.0 / 256.0)
            shift = info_ref[24 + 4 * j + r : 25 + 4 * j + r, :]
            padded = jnp.concatenate([pay[r, 64 * j : 64 * j + 64], jnp.zeros((64, 128), F32)], axis=1)
            moved = pltpu.roll(padded, turns[4 * r + j], 1)
            inside = jnp.where(lower, xs - shift, PIX - 1 - shift - xs) >= 0
            own = jnp.where(lower, h_ref[j, 0:64], h_ref[j, 64:128])
            value = jnp.where(inside, jnp.tanh(0.5 * (own - moved)), 0.0)
            value_y = value * uy
            sum0 = jnp.sum(value, axis=0, keepdims=True)
            sum1 = jnp.sum(value_y, axis=0, keepdims=True)
            sum2 = jnp.sum(value_y * uy, axis=0, keepdims=True)
            rows = (sum0, ux * sum0, sum1, ux * ux * sum0 + sum2)
            for q in range(4):
                row = jnp.where(
                    lanes == 16 * j + 4 * r + q, jnp.sum(rows[q], axis=1, keepdims=True), row
                )
    total[0] = row
    near = [
        remote(total.at[0], rows_in.at[n], near_sems, (n,), s, (t + n) % 4) for n in range(1, 4)
    ]
    for copy in near:
        copy.start()

    for k in range(STAGES):
        for q in range(10):
            copy_of(k, q).wait_send()
    for copy in near:
        copy.wait()
    total[1] = (total[0] + rows_in[1]) + (rows_in[2] + rows_in[3])
    own = pltpu.make_async_copy(total.at[1], shared_ref.at[s], own_sems.at[2])
    own.start()

    def far(n):
        return remote(total.at[1], shared_ref.at[s], far_sems, (n,), (s + n) % N_SUB, t)

    lax.fori_loop(1, N_SUB, lambda n, c: (far(n).start(), c)[1], 0)
    for copy in sum_copies + halos:
        copy.wait()
    summed = part[b]
    for n in range(1, 8):
        summed = summed + slots[n]
    back_ref[...] = summed
    own.wait()
    lax.fori_loop(1, N_SUB, lambda n, c: (far(n).wait(), c)[1], 0)


def main(count, turns, info, heights, places, surface):
    smem = pl.BlockSpec(memory_space=pltpu.SMEM)
    vmem = pl.BlockSpec(memory_space=pltpu.VMEM)
    dma = pltpu.SemaphoreType.DMA
    return pl.pallas_call(
        functools.partial(main_kernel, count),
        out_shape=(
            jax.ShapeDtypeStruct((N_SUB, 1, 128), F32),
            jax.ShapeDtypeStruct((32, PIX), F32),
            jax.ShapeDtypeStruct((2, 8, PIX), F32),
        ),
        in_specs=[smem] + [vmem] * 6,
        out_specs=(vmem, vmem, vmem),
        scratch_shapes=[
            pltpu.VMEM((ROUNDS, 256, 384), F32),
            pltpu.VMEM((STAGES, count * 256, 384), F32),
            pltpu.VMEM((STAGES, count * 256, 384), F32),
            pltpu.VMEM((4, PART, 256), F32),
            pltpu.VMEM((4, 3, PART, 128), F32),
            pltpu.VMEM((4, 3, PART, 128), F32),
            pltpu.VMEM((4, 3, WIN, 128), F32),
            pltpu.VMEM((4, 8, 256), jnp.int32),
            pltpu.VMEM((8, 32, PIX), F32),
            pltpu.VMEM((8, 32, PIX), F32),
            pltpu.VMEM((4, 1, 128), F32),
            pltpu.VMEM((2, 1, 128), F32),
            dma((2, STAGES, 10)),
            dma((2, 4)),
            dma((2, 4)),
            dma((2, 4)),
            dma((2, 8)),
            dma((2, 2)),
            dma((2, 4)),
            dma((2, N_SUB)),
            dma((3,)),
        ],
        compiler_params=pltpu.CompilerParams(collective_id=count - 3, has_side_effects=True),
        name="main",
    )(turns, info, heights, places, surface, jnp.asarray(COL_TABLE), jnp.asarray(ROW_TABLE_T))


def swap_lanes(value, width, bit, lanes):
    swapped = jnp.where(
        (lanes & width) != 0,
        pltpu.roll(value, width, 1),
        pltpu.roll(value, 128 - width, 1),
    )
    return jnp.where(bit == 1, swapped, value)


def finish_kernel(masks, off_ref, m_ref, s_ref, back_ref, halo_ref, gc_ref, cs_ref, par_ref, out_ref):
    me, section = lax.axis_index("sub"), lax.axis_index("surf")
    lane1 = lax.broadcasted_iota(jnp.int32, (1, 128), 1)
    sub1 = lane1 // 4
    rows16 = lax.broadcasted_iota(jnp.int32, (16, 128), 0)
    lane16 = lax.broadcasted_iota(jnp.int32, (16, 128), 1)
    mask16 = jnp.zeros((16, 128), jnp.int32)
    for r in range(ROUNDS):
        mask16 = jnp.where(rows16 // 4 == r, masks[r], mask16)
    spread = (
        lax.broadcasted_iota(jnp.int32, (N_SUB, 128), 1) // 4
        == lax.broadcasted_iota(jnp.int32, (N_SUB, 128), 0)
    ).astype(F32)
    table = lax.dot_general(
        m_ref[:, 0, :], spread, (((0,), (0,)), ((), ())), precision=HIGH, preferred_element_type=F32
    )
    own = jnp.zeros((16, 128), F32)
    place = jnp.zeros((8, 128), F32)
    for j in range(4):
        own = jnp.where(lane16 % 4 == j, table[16 * j : 16 * j + 16], own)
        place = jnp.where(lane16[:8] % 4 == j, table[64 + 8 * j : 72 + 8 * j], place)
    other = own
    shifts = off_ref[...]
    mask4 = jnp.concatenate([mask16[4 * r : 4 * r + 1] for r in range(ROUNDS)], axis=0)
    lane4 = lane16[:4]
    other_shift = shifts
    for bit in range(5):
        other = swap_lanes(other, 4 << bit, (mask16 >> bit) & 1, lane16)
        other_shift = swap_lanes(other_shift, 4 << bit, (mask4 >> bit) & 1, lane4)
    lower4 = (lane4 // 4) < jnp.bitwise_xor(lane4 // 4, mask4)
    shifts = jnp.where(lower4, shifts, other_shift)
    delta = jnp.where(lower4, shifts, -shifts).astype(F32) * (1.0 / 256.0)
    rhs = [jnp.zeros((1, 128), F32) for _ in range(4)]
    for r in range(ROUNDS):
        o = [own[4 * r + k : 4 * r + k + 1] for k in range(4)]
        p = [other[4 * r + k : 4 * r + k + 1] for k in range(4)]
        d = delta[r : r + 1]
        rhs[0] = rhs[0] + (o[0] - p[0])
        rhs[1] = rhs[1] + (o[1] - (p[1] + d * p[0]))
        rhs[2] = rhs[2] + (o[2] - p[2])
        rhs[3] = rhs[3] + (o[3] - (p[3] + d * (2.0 * p[1] + d * p[0])))
    column = lax.broadcasted_iota(jnp.int32, (PIX, 128), 0)
    count = jnp.zeros((PIX, 128), F32)
    for r in range(ROUNDS):
        shift = shifts[r : r + 1]
        low = jnp.where(lower4[r : r + 1], shift, 0)
        high = jnp.where(lower4[r : r + 1], PIX, PIX - shift)
        count = count + jnp.where((column >= low) & (column < high), 1.0, 0.0)
    ux = (lax.broadcasted_iota(jnp.int32, (PIX, 1), 0).astype(F32) - 255.5) * (1.0 / 256.0)
    power = []
    term = count
    for k in range(5):
        power.append(jnp.sum(term, axis=0, keepdims=True))
        if k < 4:
            term = term * ux
    y0, y2, y4 = _ROW_U2[0], _ROW_U2[2], _ROW_U2[4]
    g00 = power[0] * y0
    g01 = power[1] * y0
    g03 = power[2] * y0 + power[0] * y2
    g11 = power[2] * y0
    g13 = power[3] * y0 + power[1] * y2
    g22 = power[0] * y2
    g33 = power[4] * y0 + 2.0 * power[2] * y2 + power[0] * y4
    l00 = jnp.sqrt(g00)
    l10 = g01 / l00
    l30 = g03 / l00
    l11 = jnp.sqrt(g11 - l10 * l10)
    l31 = (g13 - l30 * l10) / l11
    l33 = jnp.sqrt(g33 - l30 * l30 - l31 * l31)
    z0 = rhs[0] / l00
    z1 = (rhs[1] - l10 * z0) / l11
    z3 = (rhs[3] - l30 * z0 - l31 * z1) / l33
    p3 = z3 / l33
    p1 = (z1 - l31 * p3) / l11
    p0 = (z0 - l10 * p1 - l30 * p3) / l00
    p2 = rhs[2] / g22
    params = jnp.concatenate([p0, p1, p2, p3], axis=0)
    par_ref[...] = pltpu.roll(params, (128 - 4 * me) % 128, 1)[:, 0:4]
    start = place[1:2].astype(jnp.int32)
    a = lax.broadcasted_iota(jnp.int32, (32, 128), 0) + 32 * me - start
    in_window = (a >= 0) & (a < N_COEF)
    middle = (a > EDGES[2]) & (a < EDGES[3])
    edges = [(a == e).astype(F32) for e in EDGES]

    def quantity(q, inner):
        value = jnp.where(middle, inner, 0.0)
        for e, at in zip(EDGES, edges):
            if _QUANT[e, q] != 0.0:
                value = value + at * float(_QUANT[e, q])
        return value

    centre = (4.0 * (a.astype(F32) - 1.0) - 255.5) * (1.0 / 256.0)
    bands = [quantity(q, float(_MID[q])) for q in range(7)]
    sum0 = quantity(7, 4.0)
    sum1 = quantity(8, 4.0 * centre)
    sum2 = quantity(9, 4.0 * centre * centre + _VAR)
    plane0 = p0 * sum0 + p2 * sum1 + p3 * sum2
    plane1 = p1 * sum0
    plane2 = p3 * sum0
    out_ref[...] = back_ref[...]
    weight = [jnp.zeros((32, 128), F32) for _ in range(4)]
    for c in range(3):
        chosen = (place[0:1] == section.astype(F32)) & (place[2:3] == float(c))
        chosen = chosen.astype(F32)
        band = [jnp.sum(v * chosen, axis=1, keepdims=True) for v in bands]
        plane = [jnp.sum(v * chosen, axis=1, keepdims=True) for v in (plane0, plane1, plane2)]
        cols = pl.ds(128 * c, 256)
        tall = jnp.concatenate([halo_ref[0, :, cols], s_ref[:, cols], halo_ref[1, :, cols]], axis=0)
        normal = jnp.dot(tall, gc_ref[...], precision=HIGH, preferred_element_type=F32)
        taken = plane[0] * cs_ref[0:1] + plane[1] * cs_ref[1:2] + plane[2] * cs_ref[2:3]
        for d in range(-BAND, BAND + 1):
            taken = taken + band[d + BAND] * normal[8 + d : 40 + d]
        out_ref[:, cols] = out_ref[:, cols] - taken
        diag = band[BAND] * cs_ref[3:4]
        weight[c] = weight[c] + diag[:, :128]
        weight[c + 1] = weight[c + 1] + diag[:, 128:]
    for c in range(4):
        cols = pl.ds(128 * c, 128)
        out_ref[:, cols] = s_ref[:, cols] + out_ref[:, cols] / (weight[c] + 1.0)


def finish(masks, offsets, shared, surface, back, halo):
    vmem = pl.BlockSpec(memory_space=pltpu.VMEM)
    return pl.pallas_call(
        finish_kernel,
        out_shape=(jax.ShapeDtypeStruct((4, 4), F32), jax.ShapeDtypeStruct((32, 512), F32)),
        in_specs=[pl.BlockSpec(memory_space=pltpu.SMEM)] + [vmem] * 7,
        out_specs=(vmem, vmem),
        name="finish",
    )(masks, offsets, shared, surface, back, halo, jnp.asarray(COL_NORMAL), jnp.asarray(COL_SUMS))


def per_device(heights, masks, offsets, sections, row_starts, col_blocks, surface):
    info, turns, places, fits = setup(masks, offsets, sections.reshape(4), row_starts, col_blocks)
    shared, back, halo = lax.cond(
        fits[0] == 1,
        functools.partial(main, 3),
        functools.partial(main, 4),
        turns,
        info,
        heights,
        places,
        surface,
    )
    params, fitted = finish(masks, offsets, shared, surface, back, halo)
    return params, fitted


def solution(mesh):
    in_specs = (
        P("sub", "surf", None),
        P(),
        P(),
        P("sub", None),
        P("sub"),
        P("sub"),
        P("sub", "surf"),
    )
    out_specs = (P(None, "sub"), P("sub", "surf"))
    return jax.shard_map(
        per_device, mesh=mesh, in_specs=in_specs, out_specs=out_specs, check_vma=False
    )
```
